32 devices in a mesh: groups: 2 (over y), visits: 16 (over z, x, core).
Axes of the slice: x: 2, y: 2, z: 4, core: 2. Of those that a mesh axis runs over, the one named last changes fastest.
Arguments:
- exposure: float32 [224, 8, 128], P(('groups', 'visits')), parts along dimension 0, may hold values from -6 to 6
- patch_of: int32 [224], P(('groups', 'visits')), parts along dimension 0, may hold values from -1 to 15, as said below
- affine: int32 [6, 224], P(None, ('groups', 'visits')), parts along dimension 1, may hold values from -2048 to 2048, as said below
- psf_weights: float32 [2, 4, 224], P(None, None, ('groups', 'visits')), parts along dimension 2, may hold values from 0.25 to 1
- psf_basis: float32 [2, 4, 21], replicated, may hold values from -2 to 2
- detect_taps: float32 [2, 21], replicated, may hold values from -2 to 2
Outputs:
- template: bfloat16 [32, 8, 128], P(('groups', 'visits')), parts along dimension 0
- difference: float32 [224, 8, 128], P(('groups', 'visits')), parts along dimension 0
- detection: float32 [224, 8, 128], P(('groups', 'visits')), parts along dimension 0
The draws below stay inside these ranges and needn't reach their ends.
There are 2 independent parts, one for each index of `groups`. The reference program is written for one: setup_inputs(seed, part) draws one part's arguments, and reference() takes and returns one part's arrays. A program takes and returns all parts, laid end to end along the dimension named above; an argument that names none is the same for every part. Nothing has to cross between parts.
Inputs may be any that keep to these rules, and one draw needn't show every extreme that they name: `patch_of`: within the slots of one visit no patch appears twice. Every patch is intersected by between 3 and 16 tile slots, and in every draw some patch by exactly 16 and some by exactly 3. `affine`: rows 0 and 4 lie in 240 to 272, rows 1 and 3 in -16 to 16, row 2 in -128 to 128, row 5 in -2048 to 2048.
All inputs are finite; a program needn't handle non-finite values.
Results may differ from the reference program's by a relative error of at most 0.0039.
Values may be sent and summed in bfloat16 or wider, within the bound.
No kernel may reach another device: no remote copies, remote signals or barrier semaphores. Data moves between devices by JAX's collectives and lax.ppermute only.
A program may use at most 64 MiB of HBM per device.

```python
import jax
import jax.numpy as jnp
from jax import lax

TILE = 128
TROWS = 8
KW = 21
RANK = 4
PATCHES = 16
MAXCNT = 16
MINCNT = 3
TSLOT = 7
EXPOS = 112


def draw_patch_of(key, part):
    base = jax.random.fold_in(key, 7)
    count_key, order_key = jax.random.split(base, 2)
    spread = jax.random.randint(count_key, (PATCHES,), 0, MINCNT + 1)
    members = MINCNT + spread
    members = members.at[0].set(MAXCNT)
    members = members.at[1].set(MINCNT)
    members = members.astype(jnp.int32)
    ordering = jax.random.permutation(order_key, PATCHES).astype(jnp.int32)
    bounds = jnp.cumsum(members).astype(jnp.int32)
    positions = jnp.arange(PATCHES * TSLOT, dtype=jnp.int32)
    slot_list = jnp.sum((bounds[None, :] <= positions[:, None]).astype(jnp.int32), axis=1)
    patch_ids = jnp.where(positions < bounds[-1], ordering[jnp.minimum(slot_list, PATCHES - 1)], -1)
    return patch_ids.reshape(TSLOT, PATCHES).T.reshape(-1).astype(jnp.int32)


def draw_affine(key, part):
    base = jax.random.fold_in(key, 13)
    lowest = jnp.array([240, -16, -16 * TROWS, -16, 240, -16 * TILE], jnp.int32)
    highest = jnp.array([273, 17, 16 * TROWS + 1, 17, 273, 16 * TILE + 1], jnp.int32)
    return jax.random.randint(base, (6, EXPOS), lowest[:, None], highest[:, None]).astype(jnp.int32)


def steps_of(key, shape, cuts, least, top_value):
    level = 1.0
    for position, parts in cuts:
        draws = jax.random.uniform(jax.random.fold_in(jax.random.fold_in(key, 6), position), (parts,), jnp.float32, least / len(cuts), top_value / len(cuts))
        level = level * jnp.repeat(jnp.exp(draws), shape[position] // parts).reshape((-1,) + (1,) * (len(shape) - 1 - position))
    return level


def scatter_about(key, shape, scale, limit, cuts=(), held_as=jnp.bfloat16):
    entries = jax.random.normal(key, shape, jnp.float32) * scale
    if len(cuts) > 0:
        entries = steps_of(key, shape, cuts, -0.22, 0.18) * entries
    return jnp.clip(entries, min=-limit, max=limit).astype(held_as)


def setup_inputs(seed: int = 0, part: int = 0) -> dict:
    splits = jax.random.split(jax.random.key(seed), 7)
    part_keys = jax.random.split(jax.random.fold_in(splits[6], part), 7)
    return {
        "exposure": scatter_about(part_keys[0], (EXPOS, TROWS, TILE), 1.0, 6.0, ((0, 16),), jnp.float32),
        "patch_of": draw_patch_of(jax.random.fold_in(jax.random.fold_in(splits[6], part), 71), part),
        "affine": draw_affine(jax.random.fold_in(jax.random.fold_in(splits[6], part), 71), part),
        "psf_weights": jnp.clip(0.25 + 0.75 * jax.random.uniform(part_keys[3], (2, RANK, EXPOS), jnp.float32) ** steps_of(part_keys[3], (2, RANK, EXPOS), ((2, 16),), -0.2, 0.2), 0.25, 1.0),
        "psf_basis": scatter_about(splits[4], (2, RANK, KW), 0.35, 2.0, (), jnp.float32),
        "detect_taps": scatter_about(splits[5], (2, KW), 0.35, 2.0, (), jnp.float32),
    }


def band_stack(kernel, extent):
    taps = kernel.shape[-1]
    centre = (taps - 1) // 2
    row_ids = jnp.arange(extent, dtype=jnp.int32)[:, None]
    col_ids = jnp.arange(extent, dtype=jnp.int32)[None, :]
    offset = col_ids - row_ids + centre
    select = (offset[None] == jnp.arange(taps, dtype=jnp.int32)[:, None, None]).astype(jnp.float32)
    return jnp.einsum('kd,dim->kim', kernel, select, precision=lax.Precision.HIGHEST)


def apply_filter(field, weights, row_taps, col_taps):
    row_band = band_stack(row_taps, field.shape[-2])
    col_band = band_stack(col_taps, field.shape[-1])
    total = jnp.zeros(field.shape, jnp.float32)
    for term in range(row_taps.shape[0]):
        partial_value = jnp.einsum('ein,jn->eij', field, col_band[term], precision=lax.Precision.HIGHEST)
        shaped = jnp.einsum('im,emj->eij', row_band[term], partial_value, precision=lax.Precision.HIGHEST)
        total = total + weights[term][:, None, None] * shaped
    return total


def warp_tiles(exposure, affine):
    height = exposure.shape[-2]
    extent = exposure.shape[-1]
    tiles = exposure.shape[0]
    row_ids = jnp.arange(height, dtype=jnp.int32)[None, :, None]
    col_ids = jnp.arange(extent, dtype=jnp.int32)[None, None, :]
    coeffs = affine.astype(jnp.int32)[:, :, None, None]
    src_row = jnp.clip((coeffs[0] * row_ids + coeffs[1] * col_ids + coeffs[2]) // 256, 0, height - 1)
    src_col = jnp.clip((coeffs[3] * row_ids + coeffs[4] * col_ids + coeffs[5]) // 256, 0, extent - 1)
    source = (src_row * extent + src_col).reshape(tiles, -1).astype(jnp.int32)
    flat = jnp.take_along_axis(exposure.reshape(tiles, -1), source, axis=1)
    return flat.reshape(exposure.shape)


def reference(exposure, patch_of, affine, psf_weights, psf_basis, detect_taps):
    tiles = exposure.shape[0]
    warped = warp_tiles(exposure, affine)
    matched = apply_filter(warped, psf_weights[0], psf_basis[0], psf_basis[1]).astype(jnp.bfloat16)
    onehot = (patch_of[:, None] == jnp.arange(PATCHES, dtype=jnp.int32)[None, :]).astype(jnp.int32)
    before = (jnp.cumsum(onehot, axis=0) - onehot).astype(jnp.int32)
    order_in = jnp.sum(before * onehot, axis=1).astype(jnp.int32)
    members = jnp.sum(onehot, axis=0).astype(jnp.int32)
    target = jnp.where(patch_of >= 0, patch_of, PATCHES).astype(jnp.int32)
    roster = jnp.zeros((PATCHES, MAXCNT), jnp.int32).at[target, order_in].set(
        jnp.arange(tiles, dtype=jnp.int32), mode='drop')

    def patch_median(pair):
        indices, count_here = pair
        values = matched[indices]
        is_live = jnp.arange(MAXCNT, dtype=jnp.int32) < count_here
        values = jnp.where(is_live[:, None, None], values, jnp.array(jnp.inf, values.dtype))
        ordered = jnp.sort(values, axis=0)
        lower = lax.dynamic_index_in_dim(ordered, (count_here - 1) // 2, 0, keepdims=False).astype(jnp.float32)
        upper = lax.dynamic_index_in_dim(ordered, count_here // 2, 0, keepdims=False).astype(jnp.float32)
        return ((lower + upper) * 0.5).astype(jnp.bfloat16)

    template = lax.map(patch_median, (roster, members))
    own_template = template[jnp.clip(patch_of, 0, PATCHES - 1)].astype(jnp.float32)
    modelled = apply_filter(own_template, psf_weights[1], psf_basis[0], psf_basis[1])
    covered = (patch_of >= 0)[:, None, None]
    difference = jnp.where(covered, warped - modelled, jnp.zeros_like(warped))
    detection = apply_filter(difference, jnp.ones((1, tiles), jnp.float32), detect_taps[0:1], detect_taps[1:2])
    return template, difference, detection
```

```python
import jax
import jax.numpy as jnp
from jax import lax
from jax.experimental import pallas as pl
from jax.experimental.pallas import tpu as pltpu
from jax.sharding import PartitionSpec as P

CHUNK = 7
UNROLL_LIMIT = 2048


def round_up(value, step):
    return -(-value // step) * step


def block_rows(tiles, height):
    return round_up(tiles * height + round_up(tiles, height), 2 * height)


def tap_filter(strips, rank, taps, row_tap, col_tap, weight):
    height, extent = strips[0].shape
    centre = (taps - 1) // 2
    cols = lax.broadcasted_iota(jnp.int32, (height, extent), 1)
    rows = lax.broadcasted_iota(jnp.int32, (height, extent), 0)
    partial = [[None] * rank for _ in strips]
    for q in range(taps):
        reach = q - centre
        if abs(reach) >= extent:
            continue
        scale = [col_tap(k, q) for k in range(rank)]
        inside = (cols + reach >= 0) & (cols + reach < extent)
        if reach > 0:
            inside = cols < extent - reach
        elif reach < 0:
            inside = cols >= -reach
        for e, strip in enumerate(strips):
            moved = strip
            if reach != 0:
                moved = jnp.where(inside, pltpu.roll(strip, (-reach) % extent, 1), 0.0)
            for k in range(rank):
                term = scale[k] * moved
                partial[e][k] = term if partial[e][k] is None else partial[e][k] + term
    if weight is not None:
        partial = [[weight(k, e) * partial[e][k] for k in range(rank)] for e in range(len(strips))]
    totals = [None] * len(strips)
    for p in range(taps):
        reach = p - centre
        if abs(reach) >= height:
            continue
        scale = [row_tap(k, p) for k in range(rank)]
        if reach > 0:
            inside = rows < height - reach
        else:
            inside = rows >= -reach
        for e in range(len(strips)):
            mixed = scale[0] * partial[e][0]
            for k in range(1, rank):
                mixed = mixed + scale[k] * partial[e][k]
            if reach != 0:
                mixed = jnp.where(inside, pltpu.roll(mixed, (-reach) % height, 0), 0.0)
            totals[e] = mixed if totals[e] is None else totals[e] + mixed
    return totals


def warp_strip(strip, coeff):
    height, extent = strip.shape
    rows = lax.broadcasted_iota(jnp.int32, (height, extent), 0)
    cols = lax.broadcasted_iota(jnp.int32, (height, extent), 1)
    src_row = jnp.clip((coeff(0) * rows + coeff(1) * cols + coeff(2)) >> 8, 0, height - 1)
    src_col = jnp.clip((coeff(3) * rows + coeff(4) * cols + coeff(5)) >> 8, 0, extent - 1)
    warped = jnp.zeros_like(strip)
    for r in range(height):
        line = jnp.broadcast_to(strip[r : r + 1, :], (height, extent))
        picked = jnp.take_along_axis(line, src_col, axis=1, mode="promise_in_bounds")
        warped = jnp.where(src_row == r, picked, warped)
    return warped


def match_kernel(exposure, patch_of, affine, psf_weights, psf_basis, warped_out, block_out):
    tiles, height, extent = exposure.shape
    rank, taps = psf_basis.shape[1:]
    pieces = []
    for first in range(0, tiles, CHUNK):
        chunk = range(first, min(first + CHUNK, tiles))
        strips = []
        for e in chunk:
            strips.append(warp_strip(exposure[e], lambda row, e=e: affine[row, e]))
            warped_out[e] = strips[-1]
        pieces += tap_filter(
            strips,
            rank,
            taps,
            lambda k, p: psf_basis[0, k, p],
            lambda k, q: psf_basis[1, k, q],
            lambda k, i, first=first: psf_weights[0, k, first + i],
        )
    rows = lax.broadcasted_iota(jnp.int32, (height, extent), 0)
    for first in range(0, tiles, height):
        ids = jnp.full((height, extent), -1, jnp.int32)
        for t in range(first, min(first + height, tiles)):
            ids = jnp.where(rows == t - first, patch_of[t], ids)
        pieces.append(ids.astype(jnp.float32))
    while len(pieces) * height < block_out.shape[0]:
        pieces.append(jnp.full((height, extent), -1.0, jnp.float32))
    for i in range(0, len(pieces), 2):
        pair = jnp.concatenate(pieces[i : i + 2], axis=0)
        block_out[i * height : (i + 2) * height, :] = pair.astype(jnp.bfloat16)


def sorting_pairs(count):
    pairs = []
    p = 1
    while p < count:
        k = p
        while k >= 1:
            for j in range(k % p, count - k, 2 * k):
                for i in range(min(k, count - j - k)):
                    if (i + j) // (2 * p) == (i + j + k) // (2 * p):
                        pairs.append((i + j, i + j + k))
            k //= 2
        p *= 2
    return pairs


def median_of(candidates):
    far = jnp.full(candidates[0].shape, jnp.inf, jnp.float32)
    fill = far
    values = []
    for value in candidates:
        missing = value == far
        values.append(jnp.where(missing, fill, value))
        fill = jnp.where(missing, -fill, fill)
    count = len(values)
    for low, high in sorting_pairs(count):
        a, b = values[low], values[high]
        values[low], values[high] = jnp.minimum(a, b), jnp.maximum(a, b)
    lower, upper = values[count // 2 - 1], values[count // 2]
    upper = jnp.where(fill == far, upper, lower)
    return ((lower + upper) * 0.5).astype(jnp.bfloat16).astype(jnp.float32)


def coadd_kernel(n_pieces, *refs):
    blocks = refs[:n_pieces]
    patch_of, psf_weights, psf_basis, detect_taps, warped = refs[n_pieces : n_pieces + 5]
    template_out, difference_out, detection_out, held, models = refs[n_pieces + 5 :]
    tiles, height, extent = warped.shape
    rank, taps = psf_basis.shape[1:]
    rows_each = block_rows(tiles, height)
    me = lax.axis_index("visits")
    visits = held.shape[1]

    def strips_of(block, at):
        parts = []
        for i in range(0, rows_each // height, 2):
            pair = block[pl.ds(at + i * height, 2 * height), :].astype(jnp.float32)
            parts += [pair[:height], pair[height:]]
        return parts[:tiles], parts[tiles:]

    def gather_candidates(block, at, targets):
        strips, ids = strips_of(block, at)
        found = [jnp.full((height, extent), jnp.inf, jnp.float32) for _ in targets]
        for t in range(tiles):
            row = t % height
            label = jnp.broadcast_to(ids[t // height][row : row + 1, :], (height, extent))
            for g, target in enumerate(targets):
                found[g] = jnp.where(label == target, strips[t], found[g])
        return found

    def as_target(patch):
        return jnp.full((height, extent), patch, jnp.int32).astype(jnp.float32)

    if visits * tiles * (tiles + 1) <= UNROLL_LIMIT:
        targets = [as_target(patch_of[t]) for t in range(tiles)] + [as_target(me)]
        slot = 0
        for block in blocks:
            for b in range(block.shape[0] // rows_each):
                found = gather_candidates(block, b * rows_each, targets)
                for g in range(tiles + 1):
                    held[g, slot] = found[g]
                slot += 1
        for g in range(tiles + 1):
            models[g] = median_of([held[g, s] for s in range(visits)])
    else:

        def each_target(g, carry):
            patch = jnp.where(g < tiles, patch_of[jnp.minimum(g, tiles - 1)], me)
            target = [as_target(patch)]
            start = 0
            for block in blocks:
                count = block.shape[0] // rows_each

                def each_block(b, inner, block=block, start=start):
                    at = pl.multiple_of(b * rows_each, 2 * height)
                    held[0, start + b] = gather_candidates(block, at, target)[0]
                    return inner

                lax.fori_loop(0, count, each_block, 0)
                start += count
            models[g] = median_of([held[0, s] for s in range(visits)])
            return carry

        lax.fori_loop(0, tiles + 1, each_target, 0)

    template_out[0] = models[tiles].astype(jnp.bfloat16)
    for first in range(0, tiles, CHUNK):
        chunk = range(first, min(first + CHUNK, tiles))
        modelled = tap_filter(
            [models[e] for e in chunk],
            rank,
            taps,
            lambda k, p: psf_basis[0, k, p],
            lambda k, q: psf_basis[1, k, q],
            lambda k, i, first=first: psf_weights[1, k, first + i],
        )
        rest = []
        for i, e in enumerate(chunk):
            present = jnp.full((height, extent), patch_of[e], jnp.int32) >= 0
            rest.append(jnp.where(present, warped[e] - modelled[i], 0.0))
            difference_out[e] = rest[-1]
        detected = tap_filter(
            rest,
            1,
            taps,
            lambda k, p: detect_taps[0, p],
            lambda k, q: detect_taps[1, q],
            None,
        )
        for i, e in enumerate(chunk):
            detection_out[e] = detected[i]


def gather_blocks(block, visits):
    if visits & (visits - 1):
        return [lax.all_gather(block, "visits", axis=0, tiled=True)]
    masks = []
    bit = visits // 2
    while bit >= 1:
        masks.append(bit | 1)
        bit //= 2
    pieces = [block]
    for mask in masks:
        held = pieces[0] if len(pieces) == 1 else jnp.concatenate(pieces, axis=0)
        partner = [(i, i ^ mask) for i in range(visits)]
        pieces = [held, lax.ppermute(held, "visits", partner)]
    return pieces


def shards(exposure, patch_of, affine, psf_weights, psf_basis, detect_taps):
    visits = lax.axis_size("visits")
    tiles, height, extent = exposure.shape
    if visits > 256 or visits & (visits - 1):
        raise ValueError("visits")
    vmem = pl.BlockSpec(memory_space=pltpu.VMEM)
    smem = pl.BlockSpec(memory_space=pltpu.SMEM)
    rows = block_rows(tiles, height)
    warped, block = pl.pallas_call(
        match_kernel,
        name="match",
        out_shape=(
            jax.ShapeDtypeStruct(exposure.shape, jnp.float32),
            jax.ShapeDtypeStruct((rows, extent), jnp.bfloat16),
        ),
        in_specs=[vmem, smem, smem, smem, smem],
        out_specs=(vmem, vmem),
    )(exposure, patch_of, affine, psf_weights, psf_basis)
    pieces = gather_blocks(block, visits)
    held_targets = tiles + 1 if visits * tiles * (tiles + 1) <= UNROLL_LIMIT else 1
    template, difference, detection = pl.pallas_call(
        lambda *refs: coadd_kernel(len(pieces), *refs),
        name="coadd",
        out_shape=(
            jax.ShapeDtypeStruct((1, height, extent), jnp.bfloat16),
            jax.ShapeDtypeStruct(exposure.shape, jnp.float32),
            jax.ShapeDtypeStruct(exposure.shape, jnp.float32),
        ),
        in_specs=[vmem] * len(pieces) + [smem, smem, smem, smem, vmem],
        out_specs=(vmem, vmem, vmem),
        scratch_shapes=[
            pltpu.VMEM((held_targets, visits, height, extent), jnp.float32),
            pltpu.VMEM((tiles + 1, height, extent), jnp.float32),
        ],
    )(*pieces, patch_of, psf_weights, psf_basis, detect_taps, warped)
    return (template, difference, detection)


def solution(mesh):
    placed = (
        P(("groups", "visits"), None, None),
        P(("groups", "visits")),
        P(None, ("groups", "visits")),
        P(None, None, ("groups", "visits")),
        P(),
        P(),
    )
    return jax.shard_map(
        shards,
        mesh=mesh,
        in_specs=placed,
        out_specs=(
            P(("groups", "visits"), None, None),
            P(("groups", "visits"), None, None),
            P(("groups", "visits"), None, None),
        ),
        check_vma=False,
    )
```

```python
import jax
import jax.numpy as jnp
from jax import lax
from jax.experimental import pallas as pl
from jax.experimental.pallas import tpu as pltpu
from jax.sharding import PartitionSpec as P

CHUNK = 7
UNROLL_LIMIT = 2048
ON_CHIP_LIMIT = 1 << 19


def round_up(value, step):
    return -(-value // step) * step


def block_rows(tiles, height):
    return round_up(tiles * height + round_up(tiles, height), 2 * height)


def tap_filter(strips, rank, taps, row_tap, col_tap, weight):
    height, extent = strips[0].shape
    centre = (taps - 1) // 2
    cols = lax.broadcasted_iota(jnp.int32, (height, extent), 1)
    rows = lax.broadcasted_iota(jnp.int32, (height, extent), 0)
    partial = [[None] * rank for _ in strips]
    for q in range(taps):
        reach = q - centre
        if abs(reach) >= extent:
            continue
        scale = [col_tap(k, q) for k in range(rank)]
        inside = cols < extent - reach if reach > 0 else cols >= -reach
        for e, strip in enumerate(strips):
            moved = strip
            if reach != 0:
                moved = jnp.where(inside, pltpu.roll(strip, (-reach) % extent, 1), 0.0)
            for k in range(rank):
                term = scale[k] * moved
                partial[e][k] = term if partial[e][k] is None else partial[e][k] + term
    if weight is not None:
        partial = [[weight(k, e) * partial[e][k] for k in range(rank)] for e in range(len(strips))]
    totals = [None] * len(strips)
    for p in range(taps):
        reach = p - centre
        if abs(reach) >= height:
            continue
        scale = [row_tap(k, p) for k in range(rank)]
        inside = rows < height - reach if reach > 0 else rows >= -reach
        for e in range(len(strips)):
            mixed = scale[0] * partial[e][0]
            for k in range(1, rank):
                mixed = mixed + scale[k] * partial[e][k]
            if reach != 0:
                mixed = jnp.where(inside, pltpu.roll(mixed, (-reach) % height, 0), 0.0)
            totals[e] = mixed if totals[e] is None else totals[e] + mixed
    return totals


def warp_strip(strip, coeff):
    height, extent = strip.shape
    rows = lax.broadcasted_iota(jnp.int32, (height, extent), 0)
    cols = lax.broadcasted_iota(jnp.int32, (height, extent), 1)
    src_row = jnp.clip((coeff(0) * rows + coeff(1) * cols + coeff(2)) >> 8, 0, height - 1)
    src_col = jnp.clip((coeff(3) * rows + coeff(4) * cols + coeff(5)) >> 8, 0, extent - 1)
    warped = jnp.zeros_like(strip)
    for r in range(height):
        line = jnp.broadcast_to(strip[r : r + 1, :], (height, extent))
        picked = jnp.take_along_axis(line, src_col, axis=1, mode="promise_in_bounds")
        warped = jnp.where(src_row == r, picked, warped)
    return warped


def match_kernel(exposure, patch_of, affine, psf_weights, psf_basis, warped_out, block_out):
    tiles, height, extent = exposure.shape
    rank, taps = psf_basis.shape[1:]
    pieces = []
    for first in range(0, tiles, CHUNK):
        chunk = range(first, min(first + CHUNK, tiles))
        strips = []
        for e in chunk:
            strips.append(warp_strip(exposure[e], lambda row, e=e: affine[row, e]))
            warped_out[e] = strips[-1]
        pieces += tap_filter(
            strips,
            rank,
            taps,
            lambda k, p: psf_basis[0, k, p],
            lambda k, q: psf_basis[1, k, q],
            lambda k, i, first=first: psf_weights[0, k, first + i],
        )
    rows = lax.broadcasted_iota(jnp.int32, (height, extent), 0)
    for first in range(0, tiles, height):
        ids = jnp.full((height, extent), -1, jnp.int32)
        for t in range(first, min(first + height, tiles)):
            ids = jnp.where(rows == t - first, patch_of[t], ids)
        pieces.append(ids.astype(jnp.float32))
    while len(pieces) * height < block_out.shape[0]:
        pieces.append(jnp.full((height, extent), -1.0, jnp.float32))
    for i in range(0, len(pieces), 2):
        pair = jnp.concatenate(pieces[i : i + 2], axis=0)
        block_out[i * height : (i + 2) * height, :] = pair.astype(jnp.bfloat16)


def sorting_pairs(count):
    pairs = []
    p = 1
    while p < count:
        k = p
        while k >= 1:
            for j in range(k % p, count - k, 2 * k):
                for i in range(min(k, count - j - k)):
                    if (i + j) // (2 * p) == (i + j + k) // (2 * p):
                        pairs.append((i + j, i + j + k))
            k //= 2
        p *= 2
    return pairs


def median_of(candidates):
    far = jnp.full(candidates[0].shape, jnp.inf, jnp.float32)
    fill = far
    values = []
    for value in candidates:
        missing = value == far
        values.append(jnp.where(missing, fill, value))
        fill = jnp.where(missing, -fill, fill)
    count = len(values)
    for low, high in sorting_pairs(count):
        a, b = values[low], values[high]
        values[low], values[high] = jnp.minimum(a, b), jnp.maximum(a, b)
    lower, upper = values[count // 2 - 1], values[count // 2]
    upper = jnp.where(fill == far, upper, lower)
    return ((lower + upper) * 0.5).astype(jnp.bfloat16).astype(jnp.float32)


def coadd_kernel(n_pieces, *refs):
    blocks = refs[:n_pieces]
    patch_of, psf_weights, psf_basis, detect_taps, warped = refs[n_pieces : n_pieces + 5]
    outputs = refs[n_pieces + 5 : n_pieces + 8]
    *staged, sems, held, models = refs[n_pieces + 8 :]
    template_out, difference_out, detection_out = staged
    copies = [pltpu.make_async_copy(staged[i], outputs[i], sems.at[i]) for i in range(3)]
    tiles, height, extent = warped.shape
    rank, taps = psf_basis.shape[1:]
    rows_each = block_rows(tiles, height)
    me = lax.axis_index("visits")
    visits = held.shape[1]

    def strips_of(block, at):
        parts = []
        for i in range(0, rows_each // height, 2):
            pair = block[pl.ds(at + i * height, 2 * height), :].astype(jnp.float32)
            parts += [pair[:height], pair[height:]]
        return parts[:tiles], parts[tiles:]

    def gather_candidates(block, at, targets):
        strips, ids = strips_of(block, at)
        found = [jnp.full((height, extent), jnp.inf, jnp.float32) for _ in targets]
        for t in range(tiles):
            row = t % height
            label = jnp.broadcast_to(ids[t // height][row : row + 1, :], (height, extent))
            for g, target in enumerate(targets):
                found[g] = jnp.where(label == target, strips[t], found[g])
        return found

    def as_target(patch):
        return jnp.full((height, extent), patch, jnp.int32).astype(jnp.float32)

    if visits * tiles * (tiles + 1) <= UNROLL_LIMIT:
        targets = [as_target(patch_of[t]) for t in range(tiles)] + [as_target(me)]
        slot = 0
        for block in blocks:
            for b in range(block.shape[0] // rows_each):
                found = gather_candidates(block, b * rows_each, targets)
                for g in range(tiles + 1):
                    held[g, slot] = found[g]
                slot += 1
        for g in range(tiles + 1):
            models[g] = median_of([held[g, s] for s in range(visits)])
    else:

        def each_target(g, carry):
            patch = jnp.where(g < tiles, patch_of[jnp.minimum(g, tiles - 1)], me)
            target = [as_target(patch)]
            start = 0
            for block in blocks:
                count = block.shape[0] // rows_each

                def each_block(b, inner, block=block, start=start):
                    at = pl.multiple_of(b * rows_each, 2 * height)
                    held[0, start + b] = gather_candidates(block, at, target)[0]
                    return inner

                lax.fori_loop(0, count, each_block, 0)
                start += count
            models[g] = median_of([held[0, s] for s in range(visits)])
            return carry

        lax.fori_loop(0, tiles + 1, each_target, 0)

    template_out[0] = models[tiles].astype(jnp.bfloat16)
    copies[0].start()
    for first in range(0, tiles, CHUNK):
        chunk = range(first, min(first + CHUNK, tiles))
        modelled = tap_filter(
            [models[e] for e in chunk],
            rank,
            taps,
            lambda k, p: psf_basis[0, k, p],
            lambda k, q: psf_basis[1, k, q],
            lambda k, i, first=first: psf_weights[1, k, first + i],
        )
        rest = []
        for i, e in enumerate(chunk):
            present = jnp.full((height, extent), patch_of[e], jnp.int32) >= 0
            rest.append(jnp.where(present, warped[e] - modelled[i], 0.0))
            difference_out[e] = rest[-1]
        if chunk[-1] == tiles - 1:
            copies[1].start()
        detected = tap_filter(
            rest,
            1,
            taps,
            lambda k, p: detect_taps[0, p],
            lambda k, q: detect_taps[1, q],
            None,
        )
        for i, e in enumerate(chunk):
            detection_out[e] = detected[i]
    copies[2].start()
    for copy in copies:
        copy.wait()


def gather_blocks(block, visits):
    if visits & (visits - 1):
        return [lax.all_gather(block, "visits", axis=0, tiled=True)]
    masks = []
    bit = visits // 2
    while bit >= 1:
        masks.append(bit | 1)
        bit //= 2
    pieces = [block]
    for mask in masks:
        held = pieces[0] if len(pieces) == 1 else jnp.concatenate(pieces, axis=0)
        partner = [(i, i ^ mask) for i in range(visits)]
        pieces = [held, lax.ppermute(held, "visits", partner)]
    return pieces


def on_chip(value):
    if value.size > ON_CHIP_LIMIT:
        return value
    return pltpu.with_memory_space_constraint(value, pltpu.VMEM)


def shards(exposure, patch_of, affine, psf_weights, psf_basis, detect_taps):
    visits = lax.axis_size("visits")
    tiles, height, extent = exposure.shape
    if visits > 256 or visits & (visits - 1):
        raise ValueError("visits")
    vmem = pl.BlockSpec(memory_space=pltpu.VMEM)
    smem = pl.BlockSpec(memory_space=pltpu.SMEM)
    anywhere = pl.BlockSpec(memory_space=pl.ANY)
    rows = block_rows(tiles, height)
    warped, block = pl.pallas_call(
        match_kernel,
        name="match",
        out_shape=(
            pltpu.VMEM(exposure.shape, jnp.float32),
            pltpu.VMEM((rows, extent), jnp.bfloat16),
        ),
        in_specs=[vmem, smem, smem, smem, smem],
        out_specs=(vmem, vmem),
    )(exposure, patch_of, affine, psf_weights, psf_basis)
    pieces = [on_chip(piece) for piece in gather_blocks(block, visits)]
    held_targets = tiles + 1 if visits * tiles * (tiles + 1) <= UNROLL_LIMIT else 1
    template, difference, detection = pl.pallas_call(
        lambda *refs: coadd_kernel(len(pieces), *refs),
        name="coadd",
        out_shape=(
            jax.ShapeDtypeStruct((1, height, extent), jnp.bfloat16),
            jax.ShapeDtypeStruct(exposure.shape, jnp.float32),
            jax.ShapeDtypeStruct(exposure.shape, jnp.float32),
        ),
        in_specs=[vmem] * len(pieces) + [smem, smem, smem, smem, vmem],
        out_specs=(anywhere, anywhere, anywhere),
        scratch_shapes=[
            pltpu.VMEM((1, height, extent), jnp.bfloat16),
            pltpu.VMEM(exposure.shape, jnp.float32),
            pltpu.VMEM(exposure.shape, jnp.float32),
            pltpu.SemaphoreType.DMA((3,)),
            pltpu.VMEM((held_targets, visits, height, extent), jnp.float32),
            pltpu.VMEM((tiles + 1, height, extent), jnp.float32),
        ],
    )(*pieces, patch_of, psf_weights, psf_basis, detect_taps, on_chip(warped))
    return (template, difference, detection)


def solution(mesh):
    placed = (
        P(("groups", "visits"), None, None),
        P(("groups", "visits")),
        P(None, ("groups", "visits")),
        P(None, None, ("groups", "visits")),
        P(),
        P(),
    )
    return jax.shard_map(
        shards,
        mesh=mesh,
        in_specs=placed,
        out_specs=(
            P(("groups", "visits"), None, None),
            P(("groups", "visits"), None, None),
            P(("groups", "visits"), None, None),
        ),
        check_vma=False,
    )
```

```python
import jax
import jax.numpy as jnp
from jax import lax
from jax.experimental import pallas as pl
from jax.experimental.pallas import tpu as pltpu
from jax.sharding import PartitionSpec as P

CHUNK = 7
UNROLL_LIMIT = 2048
ON_CHIP_LIMIT = 1 << 19


def round_up(value, step):
    return -(-value // step) * step


def block_rows(tiles, height):
    return round_up(tiles * height + round_up(tiles, height), 2 * height)


def reaches(taps, extent):
    centre = (taps - 1) // 2
    return [(p, p - centre) for p in range(taps) if abs(p - centre) < extent]


def col_tap_vector(value, reach, shape):
    cols = lax.broadcasted_iota(jnp.int32, shape, 1)
    inside = cols < shape[1] - reach if reach > 0 else cols >= -reach
    return jnp.where(inside, value, 0.0)


def row_tap_vector(value, reach, shape):
    rows = lax.broadcasted_iota(jnp.int32, shape, 0)
    inside = rows >= reach if reach > 0 else rows < shape[0] + reach
    return jnp.where(inside, value, 0.0)


def tap_filter(strips, rank, taps, row_tap, col_tap, weight):
    height, extent = strips[0].shape
    partial = [[None] * rank for _ in strips]
    for q, reach in reaches(taps, extent):
        scale = [col_tap(k, q, reach) for k in range(rank)]
        for e, strip in enumerate(strips):
            moved = pltpu.roll(strip, (-reach) % extent, 1) if reach else strip
            for k in range(rank):
                term = scale[k] * moved
                partial[e][k] = term if partial[e][k] is None else partial[e][k] + term
    if weight is not None:
        partial = [[weight(k, e) * partial[e][k] for k in range(rank)] for e in range(len(strips))]
    totals = [None] * len(strips)
    for p, reach in reaches(taps, height):
        scale = [row_tap(k, p, reach) for k in range(rank)]
        for e in range(len(strips)):
            mixed = scale[0] * partial[e][0]
            for k in range(1, rank):
                mixed = mixed + scale[k] * partial[e][k]
            if reach:
                mixed = pltpu.roll(mixed, (-reach) % height, 0)
            totals[e] = mixed if totals[e] is None else totals[e] + mixed
    return totals


def warp_strip(strip, coeff):
    height, extent = strip.shape
    rows = lax.broadcasted_iota(jnp.int32, (height, extent), 0)
    cols = lax.broadcasted_iota(jnp.int32, (height, extent), 1)
    src_row = jnp.clip((coeff(0) * rows + coeff(1) * cols + coeff(2)) >> 8, 0, height - 1)
    src_col = jnp.clip((coeff(3) * rows + coeff(4) * cols + coeff(5)) >> 8, 0, extent - 1)
    warped = jnp.zeros_like(strip)
    for r in range(height):
        line = jnp.broadcast_to(strip[r : r + 1, :], (height, extent))
        picked = jnp.take_along_axis(line, src_col, axis=1, mode="promise_in_bounds")
        warped = jnp.where(src_row == r, picked, warped)
    return warped


def match_kernel(exposure, patch_of, affine, psf_weights, psf_basis, warped_out, block_out):
    tiles, height, extent = exposure.shape
    rank, taps = psf_basis.shape[1:]
    pieces = []
    for first in range(0, tiles, CHUNK):
        chunk = range(first, min(first + CHUNK, tiles))
        strips = []
        for e in chunk:
            strips.append(warp_strip(exposure[e], lambda row, e=e: affine[row, e]))
            warped_out[e] = strips[-1]
        pieces += tap_filter(
            strips,
            rank,
            taps,
            lambda k, p, reach: row_tap_vector(psf_basis[0, k, p], reach, (height, extent)),
            lambda k, q, reach: col_tap_vector(psf_basis[1, k, q], reach, (height, extent)),
            lambda k, i, first=first: psf_weights[0, k, first + i],
        )
    rows = lax.broadcasted_iota(jnp.int32, (height, extent), 0)
    for first in range(0, tiles, height):
        ids = jnp.full((height, extent), -1, jnp.int32)
        for t in range(first, min(first + height, tiles)):
            ids = jnp.where(rows == t - first, patch_of[t], ids)
        pieces.append(ids.astype(jnp.float32))
    while len(pieces) * height < block_out.shape[0]:
        pieces.append(jnp.full((height, extent), -1.0, jnp.float32))
    for i in range(0, len(pieces), 2):
        pair = jnp.concatenate(pieces[i : i + 2], axis=0)
        block_out[i * height : (i + 2) * height, :] = pair.astype(jnp.bfloat16)


def sorting_pairs(count):
    pairs = []
    p = 1
    while p < count:
        k = p
        while k >= 1:
            for j in range(k % p, count - k, 2 * k):
                for i in range(min(k, count - j - k)):
                    if (i + j) // (2 * p) == (i + j + k) // (2 * p):
                        pairs.append((i + j, i + j + k))
            k //= 2
        p *= 2
    return pairs


def fill_missing(candidates, fill):
    far = jnp.full(candidates[0].shape, jnp.inf, jnp.float32)
    values = []
    for value in candidates:
        missing = value == far
        values.append(jnp.where(missing, fill, value))
        fill = jnp.where(missing, -fill, fill)
    return values, fill


def sort_values(values):
    values = list(values)
    for low, high in sorting_pairs(len(values)):
        a, b = values[low], values[high]
        values[low], values[high] = jnp.minimum(a, b), jnp.maximum(a, b)
    return values


def middle(lower, upper, fill):
    upper = jnp.where(fill > 0, upper, lower)
    return ((lower + upper) * 0.5).astype(jnp.bfloat16).astype(jnp.float32)


def median_of(candidates):
    values, fill = fill_missing(candidates, jnp.full(candidates[0].shape, jnp.inf, jnp.float32))
    values = sort_values(values)
    return middle(values[len(values) // 2 - 1], values[len(values) // 2], fill)


def block_strips(block, at, tiles, height):
    parts = []
    for i in range(0, block_rows(tiles, height) // height, 2):
        pair = block[pl.ds(at + i * height, 2 * height), :].astype(jnp.float32)
        parts += [pair[:height], pair[height:]]
    return parts[:tiles], parts[tiles:]


def gather_candidates(block, at, targets, tiles):
    height, extent = targets[0].shape
    strips, ids = block_strips(block, at, tiles, height)
    found = [jnp.full((height, extent), jnp.inf, jnp.float32) for _ in targets]
    for t in range(tiles):
        row = t % height
        label = jnp.broadcast_to(ids[t // height][row : row + 1, :], (height, extent))
        for g, target in enumerate(targets):
            found[g] = jnp.where(label == target, strips[t], found[g])
    return found


def as_target(patch, shape):
    return jnp.full(shape, patch, jnp.int32).astype(jnp.float32)


def sift_kernel(
    block, patch_of, psf_weights, psf_basis, detect_taps, ranked, fills, goals, cols, rows, weights, detect_cols, detect_rows
):
    n_targets, half, height, extent = ranked.shape
    tiles = n_targets - 1
    rank, taps = psf_basis.shape[1:]
    shape = (height, extent)
    me = lax.axis_index("visits")
    targets = [as_target(patch_of[t], shape) for t in range(tiles)] + [as_target(me, shape)]
    for g in range(n_targets):
        goals[g] = targets[g]
    rows_each = block.shape[0] // half
    for b in range(half):
        for g, value in enumerate(gather_candidates(block, b * rows_each, targets, tiles)):
            ranked[g, b] = value
    for g in range(n_targets):
        values, fill = fill_missing([ranked[g, b] for b in range(half)], jnp.full(shape, jnp.inf, jnp.float32))
        for b, value in enumerate(sort_values(values)):
            ranked[g, b] = value
        fills[g] = fill
    for q, reach in reaches(taps, extent):
        detect_cols[q] = col_tap_vector(detect_taps[1, q], reach, shape)
        for k in range(rank):
            cols[k, q] = col_tap_vector(psf_basis[1, k, q], reach, shape)
    for p, reach in reaches(taps, height):
        detect_rows[p] = row_tap_vector(detect_taps[0, p], reach, shape)
        for k in range(rank):
            rows[k, p] = row_tap_vector(psf_basis[0, k, p], reach, shape)
    for k in range(rank):
        for e in range(tiles):
            weights[k, e] = jnp.full(shape, psf_weights[1, k, e], jnp.float32)


def finish_kernel(
    block, warped, ranked, fills, goals, cols, rows, weights, detect_cols, detect_rows, *refs
):
    outputs, staged, sems, held = refs[:3], refs[3:6], refs[6], refs[7]
    template_out, difference_out, detection_out = staged
    copies = [pltpu.make_async_copy(staged[i], outputs[i], sems.at[i]) for i in range(3)]
    n_targets, half, height, extent = ranked.shape
    tiles = n_targets - 1
    rank, taps = cols.shape[:2]
    targets = [goals[g] for g in range(n_targets)]
    rows_each = block.shape[0] // half
    for b in range(half):
        for g, value in enumerate(gather_candidates(block, b * rows_each, targets, tiles)):
            held[g, b] = value
    models = []
    for g in range(n_targets):
        values, fill = fill_missing([held[g, b] for b in range(half)], fills[g])
        values = sort_values(values)
        lower, upper = None, None
        for b in range(half):
            first, second = ranked[g, b], values[half - 1 - b]
            low, high = jnp.minimum(first, second), jnp.maximum(first, second)
            lower = low if lower is None else jnp.maximum(lower, low)
            upper = high if upper is None else jnp.minimum(upper, high)
        models.append(middle(lower, upper, fill))
    template_out[0] = models[tiles].astype(jnp.bfloat16)
    copies[0].start()
    for first in range(0, tiles, CHUNK):
        chunk = range(first, min(first + CHUNK, tiles))
        modelled = tap_filter(
            [models[e] for e in chunk],
            rank,
            taps,
            lambda k, p, reach: rows[k, p],
            lambda k, q, reach: cols[k, q],
            lambda k, i, first=first: weights[k, first + i],
        )
        rest = []
        for i, e in enumerate(chunk):
            rest.append(jnp.where(targets[e] >= 0, warped[e] - modelled[i], 0.0))
            difference_out[e] = rest[-1]
        if chunk[-1] == tiles - 1:
            copies[1].start()
        detected = tap_filter(
            rest, 1, taps, lambda k, p, reach: detect_rows[p], lambda k, q, reach: detect_cols[q], None
        )
        for i, e in enumerate(chunk):
            detection_out[e] = detected[i]
    copies[2].start()
    for copy in copies:
        copy.wait()


def coadd_kernel(n_pieces, *refs):
    blocks = refs[:n_pieces]
    patch_of, psf_weights, psf_basis, detect_taps, warped = refs[n_pieces : n_pieces + 5]
    outputs = refs[n_pieces + 5 : n_pieces + 8]
    *staged, sems, held, models = refs[n_pieces + 8 :]
    template_out, difference_out, detection_out = staged
    copies = [pltpu.make_async_copy(staged[i], outputs[i], sems.at[i]) for i in range(3)]
    tiles, height, extent = warped.shape
    rank, taps = psf_basis.shape[1:]
    rows_each = block_rows(tiles, height)
    me = lax.axis_index("visits")
    visits = held.shape[0]

    def each_target(g, carry):
        patch = jnp.where(g < tiles, patch_of[jnp.minimum(g, tiles - 1)], me)
        target = [as_target(patch, (height, extent))]
        start = 0
        for block in blocks:

            def each_block(b, inner, block=block, start=start):
                at = pl.multiple_of(b * rows_each, 2 * height)
                held[start + b] = gather_candidates(block, at, target, tiles)[0]
                return inner

            count = block.shape[0] // rows_each
            lax.fori_loop(0, count, each_block, 0)
            start += count
        models[g] = median_of([held[s] for s in range(visits)])
        return carry

    lax.fori_loop(0, tiles + 1, each_target, 0)

    template_out[0] = models[tiles].astype(jnp.bfloat16)
    copies[0].start()
    for first in range(0, tiles, CHUNK):
        chunk = range(first, min(first + CHUNK, tiles))
        modelled = tap_filter(
            [models[e] for e in chunk],
            rank,
            taps,
            lambda k, p, reach: row_tap_vector(psf_basis[0, k, p], reach, (height, extent)),
            lambda k, q, reach: col_tap_vector(psf_basis[1, k, q], reach, (height, extent)),
            lambda k, i, first=first: psf_weights[1, k, first + i],
        )
        rest = []
        for i, e in enumerate(chunk):
            present = jnp.full((height, extent), patch_of[e], jnp.int32) >= 0
            rest.append(jnp.where(present, warped[e] - modelled[i], 0.0))
            difference_out[e] = rest[-1]
        if chunk[-1] == tiles - 1:
            copies[1].start()
        detected = tap_filter(
            rest,
            1,
            taps,
            lambda k, p, reach: row_tap_vector(detect_taps[0, p], reach, (height, extent)),
            lambda k, q, reach: col_tap_vector(detect_taps[1, q], reach, (height, extent)),
            None,
        )
        for i, e in enumerate(chunk):
            detection_out[e] = detected[i]
    copies[2].start()
    for copy in copies:
        copy.wait()


def gather_blocks(block, visits):
    if visits & (visits - 1):
        return [lax.all_gather(block, "visits", axis=0, tiled=True)]
    masks = []
    bit = visits // 2
    while bit >= 1:
        masks.append(bit | 1)
        bit //= 2
    pieces = [block]
    for mask in masks:
        held = pieces[0] if len(pieces) == 1 else jnp.concatenate(pieces, axis=0)
        partner = [(i, i ^ mask) for i in range(visits)]
        pieces = [held, lax.ppermute(held, "visits", partner)]
    return pieces


def on_chip(value):
    if value.size > ON_CHIP_LIMIT:
        return value
    return pltpu.with_memory_space_constraint(value, pltpu.VMEM)


def shards(exposure, patch_of, affine, psf_weights, psf_basis, detect_taps):
    visits = lax.axis_size("visits")
    tiles, height, extent = exposure.shape
    if visits > 256 or visits & (visits - 1):
        raise ValueError("visits")
    vmem = pl.BlockSpec(memory_space=pltpu.VMEM)
    smem = pl.BlockSpec(memory_space=pltpu.SMEM)
    anywhere = pl.BlockSpec(memory_space=pl.ANY)
    rows = block_rows(tiles, height)
    warped, block = pl.pallas_call(
        match_kernel,
        name="match",
        out_shape=(
            pltpu.VMEM(exposure.shape, jnp.float32),
            pltpu.VMEM((rows, extent), jnp.bfloat16),
        ),
        in_specs=[vmem, smem, smem, smem, smem],
        out_specs=(vmem, vmem),
    )(exposure, patch_of, affine, psf_weights, psf_basis)
    pieces = [on_chip(piece) for piece in gather_blocks(block, visits)]
    warped = on_chip(warped)
    results = (
        jax.ShapeDtypeStruct((1, height, extent), jnp.bfloat16),
        jax.ShapeDtypeStruct(exposure.shape, jnp.float32),
        jax.ShapeDtypeStruct(exposure.shape, jnp.float32),
    )
    scratch = [pltpu.VMEM(result.shape, result.dtype) for result in results]
    scratch.append(pltpu.SemaphoreType.DMA((3,)))
    strip = (height, extent)
    if len(pieces) != 2 or visits * tiles * (tiles + 1) > UNROLL_LIMIT:
        return pl.pallas_call(
            lambda *refs: coadd_kernel(len(pieces), *refs),
            name="coadd",
            out_shape=results,
            in_specs=[vmem] * len(pieces) + [smem, smem, smem, smem, vmem],
            out_specs=(anywhere, anywhere, anywhere),
            scratch_shapes=scratch
            + [pltpu.VMEM((visits,) + strip, jnp.float32), pltpu.VMEM((tiles + 1,) + strip, jnp.float32)],
        )(*pieces, patch_of, psf_weights, psf_basis, detect_taps, warped)
    rank, taps = psf_basis.shape[1:]
    ranked_shape = (tiles + 1, visits // 2) + strip
    sifted = pl.pallas_call(
        sift_kernel,
        name="sift",
        out_shape=tuple(
            pltpu.VMEM(shape, jnp.float32)
            for shape in (
                ranked_shape,
                (tiles + 1,) + strip,
                (tiles + 1,) + strip,
                (rank, taps) + strip,
                (rank, taps) + strip,
                (rank, tiles) + strip,
                (taps,) + strip,
                (taps,) + strip,
            )
        ),
        in_specs=[vmem, smem, smem, smem, smem],
        out_specs=(vmem,) * 8,
    )(pieces[0], patch_of, psf_weights, psf_basis, detect_taps)
    return pl.pallas_call(
        finish_kernel,
        name="finish",
        out_shape=results,
        in_specs=[vmem] * 10,
        out_specs=(anywhere, anywhere, anywhere),
        scratch_shapes=scratch + [pltpu.VMEM(ranked_shape, jnp.float32)],
    )(pieces[1], warped, *[on_chip(value) for value in sifted])


def solution(mesh):
    placed = (
        P(("groups", "visits"), None, None),
        P(("groups", "visits")),
        P(None, ("groups", "visits")),
        P(None, None, ("groups", "visits")),
        P(),
        P(),
    )
    return jax.shard_map(
        shards,
        mesh=mesh,
        in_specs=placed,
        out_specs=(
            P(("groups", "visits"), None, None),
            P(("groups", "visits"), None, None),
            P(("groups", "visits"), None, None),
        ),
        check_vma=False,
    )
```

```python
import jax
import jax.numpy as jnp
from jax import lax
from jax.experimental import pallas as pl
from jax.experimental.pallas import tpu as pltpu
from jax.sharding import PartitionSpec as P


CHUNK = 7
UNROLL_LIMIT = 2048
ON_CHIP_LIMIT = 1 << 19


def round_up(value, step):
    return -(-value // step) * step


def block_rows(tiles, height):
    return round_up(tiles * height + round_up(tiles, height), 2 * height)


def reaches(taps, extent):
    centre = (taps - 1) // 2
    return [(p, p - centre) for p in range(taps) if abs(p - centre) < extent]


def col_tap_vector(value, reach, shape):
    cols = lax.broadcasted_iota(jnp.int32, shape, 1)
    inside = cols < shape[1] - reach if reach > 0 else cols >= -reach
    return jnp.where(inside, value, 0.0)


def row_tap_vector(value, reach, shape):
    rows = lax.broadcasted_iota(jnp.int32, shape, 0)
    inside = rows >= reach if reach > 0 else rows < shape[0] + reach
    return jnp.where(inside, value, 0.0)


def tap_filter(strips, rank, taps, row_tap, col_tap, weight):
    height, extent = strips[0].shape
    partial = [[None] * rank for _ in strips]
    for q, reach in reaches(taps, extent):
        scale = [col_tap(k, q, reach) for k in range(rank)]
        for e, strip in enumerate(strips):
            moved = pltpu.roll(strip, (-reach) % extent, 1) if reach else strip
            for k in range(rank):
                term = scale[k] * moved
                partial[e][k] = term if partial[e][k] is None else partial[e][k] + term
    if weight is not None:
        partial = [[weight(k, e) * partial[e][k] for k in range(rank)] for e in range(len(strips))]
    totals = [None] * len(strips)
    for p, reach in reaches(taps, height):
        scale = [row_tap(k, p, reach) for k in range(rank)]
        for e in range(len(strips)):
            mixed = scale[0] * partial[e][0]
            for k in range(1, rank):
                mixed = mixed + scale[k] * partial[e][k]
            if reach:
                mixed = pltpu.roll(mixed, (-reach) % height, 0)
            totals[e] = mixed if totals[e] is None else totals[e] + mixed
    return totals


def warp_strip(strip, coeff):
    height, extent = strip.shape
    rows = lax.broadcasted_iota(jnp.int32, (height, extent), 0)
    cols = lax.broadcasted_iota(jnp.int32, (height, extent), 1)
    src_row = jnp.clip((coeff(0) * rows + coeff(1) * cols + coeff(2)) >> 8, 0, height - 1)
    src_col = jnp.clip((coeff(3) * rows + coeff(4) * cols + coeff(5)) >> 8, 0, extent - 1)
    warped = jnp.zeros_like(strip)
    for r in range(height):
        line = jnp.broadcast_to(strip[r : r + 1, :], (height, extent))
        picked = jnp.take_along_axis(line, src_col, axis=1, mode="promise_in_bounds")
        warped = jnp.where(src_row == r, picked, warped)
    return warped


def match_kernel(exposure, patch_of, affine, psf_weights, psf_basis, warped_out, block_out):
    tiles, height, extent = exposure.shape
    rank, taps = psf_basis.shape[1:]
    pieces = []
    for first in range(0, tiles, CHUNK):
        chunk = range(first, min(first + CHUNK, tiles))
        strips = []
        for e in chunk:
            strips.append(warp_strip(exposure[e], lambda row, e=e: affine[row, e]))
            warped_out[e] = strips[-1]
        pieces += tap_filter(
            strips,
            rank,
            taps,
            lambda k, p, reach: row_tap_vector(psf_basis[0, k, p], reach, (height, extent)),
            lambda k, q, reach: col_tap_vector(psf_basis[1, k, q], reach, (height, extent)),
            lambda k, i, first=first: psf_weights[0, k, first + i],
        )
    rows = lax.broadcasted_iota(jnp.int32, (height, extent), 0)
    for first in range(0, tiles, height):
        ids = jnp.full((height, extent), -1, jnp.int32)
        for t in range(first, min(first + height, tiles)):
            ids = jnp.where(rows == t - first, patch_of[t], ids)
        pieces.append(ids.astype(jnp.float32))
    while len(pieces) * height < block_out.shape[0]:
        pieces.append(jnp.full((height, extent), -1.0, jnp.float32))
    for i in range(0, len(pieces), 2):
        pair = jnp.concatenate(pieces[i : i + 2], axis=0)
        block_out[i * height : (i + 2) * height, :] = pair.astype(jnp.bfloat16)


def sorting_pairs(count):
    pairs = []
    p = 1
    while p < count:
        k = p
        while k >= 1:
            for j in range(k % p, count - k, 2 * k):
                for i in range(min(k, count - j - k)):
                    if (i + j) // (2 * p) == (i + j + k) // (2 * p):
                        pairs.append((i + j, i + j + k))
            k //= 2
        p *= 2
    return pairs


def fill_missing(candidates, fill):
    far = jnp.full(candidates[0].shape, jnp.inf, jnp.float32)
    values = []
    for value in candidates:
        missing = value == far
        values.append(jnp.where(missing, fill, value))
        fill = jnp.where(missing, -fill, fill)
    return values, fill


def sort_values(values):
    values = list(values)
    for low, high in sorting_pairs(len(values)):
        a, b = values[low], values[high]
        values[low], values[high] = jnp.minimum(a, b), jnp.maximum(a, b)
    return values


def middle(lower, upper, fill):
    upper = jnp.where(fill > 0, upper, lower)
    return ((lower + upper) * 0.5).astype(jnp.bfloat16).astype(jnp.float32)


def median_of(candidates):
    values, fill = fill_missing(candidates, jnp.full(candidates[0].shape, jnp.inf, jnp.float32))
    values = sort_values(values)
    return middle(values[len(values) // 2 - 1], values[len(values) // 2], fill)


def block_strips(block, at, tiles, height):
    parts = []
    for i in range(0, block_rows(tiles, height) // height, 2):
        pair = block[pl.ds(at + i * height, 2 * height), :].astype(jnp.float32)
        parts += [pair[:height], pair[height:]]
    return parts[:tiles], parts[tiles:]


def gather_candidates(block, at, targets, tiles):
    height, extent = targets[0].shape
    strips, ids = block_strips(block, at, tiles, height)
    found = [jnp.full((height, extent), jnp.inf, jnp.float32) for _ in targets]
    for t in range(tiles):
        row = t % height
        label = jnp.broadcast_to(ids[t // height][row : row + 1, :], (height, extent))
        for g, target in enumerate(targets):
            found[g] = jnp.where(label == target, strips[t], found[g])
    return found


def as_target(patch, shape):
    return jnp.full(shape, patch, jnp.int32).astype(jnp.float32)


def prep_kernel(
    patch_of, psf_weights, psf_basis, detect_taps, goals, cols, rows, weights, detect_cols, detect_rows
):
    n_targets, height, extent = goals.shape
    tiles = n_targets - 1
    rank, taps = psf_basis.shape[1:]
    shape = (height, extent)
    for t in range(tiles):
        goals[t] = as_target(patch_of[t], shape)
    goals[tiles] = as_target(lax.axis_index("visits"), shape)
    for q, reach in reaches(taps, extent):
        detect_cols[q] = col_tap_vector(detect_taps[1, q], reach, shape)
        for k in range(rank):
            cols[k, q] = col_tap_vector(psf_basis[1, k, q], reach, shape)
    for p, reach in reaches(taps, height):
        detect_rows[p] = row_tap_vector(detect_taps[0, p], reach, shape)
        for k in range(rank):
            rows[k, p] = row_tap_vector(psf_basis[0, k, p], reach, shape)
    for k in range(rank):
        for e in range(tiles):
            weights[k, e] = jnp.full(shape, psf_weights[1, k, e], jnp.float32)


def sift_kernel(block, goals, ranked, fills):
    n_targets, half, height, extent = ranked.shape
    targets = [goals[g] for g in range(n_targets)]
    rows_each = block.shape[0] // half
    for b in range(half):
        for g, value in enumerate(gather_candidates(block, b * rows_each, targets, n_targets - 1)):
            ranked[g, b] = value
    for g in range(n_targets):
        far = jnp.full((height, extent), jnp.inf, jnp.float32)
        values, fill = fill_missing([ranked[g, b] for b in range(half)], far)
        for b, value in enumerate(sort_values(values)):
            ranked[g, b] = value
        fills[g] = fill


def finish_kernel(
    block, warped, ranked, fills, goals, cols, rows, weights, detect_cols, detect_rows, *refs
):
    outputs, staged, sems, held = refs[:3], refs[3:6], refs[6], refs[7]
    template_out, difference_out, detection_out = staged
    copies = [pltpu.make_async_copy(staged[i], outputs[i], sems.at[i]) for i in range(3)]
    n_targets, half, _, _ = ranked.shape
    tiles = n_targets - 1
    rank, taps = cols.shape[:2]
    targets = [goals[g] for g in range(n_targets)]
    rows_each = block.shape[0] // half
    for b in range(half):
        for g, value in enumerate(gather_candidates(block, b * rows_each, targets, tiles)):
            held[g, b] = value
    models = []
    for g in range(n_targets):
        values, fill = fill_missing([held[g, b] for b in range(half)], fills[g])
        values = sort_values(values)
        lower, upper = None, None
        for b in range(half):
            first, second = ranked[g, b], values[half - 1 - b]
            low, high = jnp.minimum(first, second), jnp.maximum(first, second)
            lower = low if lower is None else jnp.maximum(lower, low)
            upper = high if upper is None else jnp.minimum(upper, high)
        models.append(middle(lower, upper, fill))
    template_out[0] = models[tiles].astype(jnp.bfloat16)
    copies[0].start()
    for first in range(0, tiles, CHUNK):
        chunk = range(first, min(first + CHUNK, tiles))
        modelled = tap_filter(
            [models[e] for e in chunk],
            rank,
            taps,
            lambda k, p, reach: rows[k, p],
            lambda k, q, reach: cols[k, q],
            lambda k, i, first=first: weights[k, first + i],
        )
        rest = []
        for i, e in enumerate(chunk):
            rest.append(jnp.where(targets[e] >= 0, warped[e] - modelled[i], 0.0))
            difference_out[e] = rest[-1]
        if chunk[-1] == tiles - 1:
            copies[1].start()
        detected = tap_filter(
            rest, 1, taps, lambda k, p, reach: detect_rows[p], lambda k, q, reach: detect_cols[q], None
        )
        for i, e in enumerate(chunk):
            detection_out[e] = detected[i]
    copies[2].start()
    for copy in copies:
        copy.wait()


def coadd_kernel(n_pieces, *refs):
    blocks = refs[:n_pieces]
    patch_of, psf_weights, psf_basis, detect_taps, warped = refs[n_pieces : n_pieces + 5]
    outputs = refs[n_pieces + 5 : n_pieces + 8]
    *staged, sems, held, models = refs[n_pieces + 8 :]
    template_out, difference_out, detection_out = staged
    copies = [pltpu.make_async_copy(staged[i], outputs[i], sems.at[i]) for i in range(3)]
    tiles, height, extent = warped.shape
    rank, taps = psf_basis.shape[1:]
    rows_each = block_rows(tiles, height)
    me = lax.axis_index("visits")
    visits = held.shape[0]

    def each_target(g, carry):
        patch = jnp.where(g < tiles, patch_of[jnp.minimum(g, tiles - 1)], me)
        target = [as_target(patch, (height, extent))]
        start = 0
        for block in blocks:

            def each_block(b, inner, block=block, start=start):
                at = pl.multiple_of(b * rows_each, 2 * height)
                held[start + b] = gather_candidates(block, at, target, tiles)[0]
                return inner

            count = block.shape[0] // rows_each
            lax.fori_loop(0, count, each_block, 0)
            start += count
        models[g] = median_of([held[s] for s in range(visits)])
        return carry

    lax.fori_loop(0, tiles + 1, each_target, 0)

    template_out[0] = models[tiles].astype(jnp.bfloat16)
    copies[0].start()
    for first in range(0, tiles, CHUNK):
        chunk = range(first, min(first + CHUNK, tiles))
        modelled = tap_filter(
            [models[e] for e in chunk],
            rank,
            taps,
            lambda k, p, reach: row_tap_vector(psf_basis[0, k, p], reach, (height, extent)),
            lambda k, q, reach: col_tap_vector(psf_basis[1, k, q], reach, (height, extent)),
            lambda k, i, first=first: psf_weights[1, k, first + i],
        )
        rest = []
        for i, e in enumerate(chunk):
            present = jnp.full((height, extent), patch_of[e], jnp.int32) >= 0
            rest.append(jnp.where(present, warped[e] - modelled[i], 0.0))
            difference_out[e] = rest[-1]
        if chunk[-1] == tiles - 1:
            copies[1].start()
        detected = tap_filter(
            rest,
            1,
            taps,
            lambda k, p, reach: row_tap_vector(detect_taps[0, p], reach, (height, extent)),
            lambda k, q, reach: col_tap_vector(detect_taps[1, q], reach, (height, extent)),
            None,
        )
        for i, e in enumerate(chunk):
            detection_out[e] = detected[i]
    copies[2].start()
    for copy in copies:
        copy.wait()


def gather_blocks(block, visits):
    if visits & (visits - 1):
        return [lax.all_gather(block, "visits", axis=0, tiled=True)]
    pieces = [block]
    for masks in exchange_stages(visits):
        held = pieces[0] if len(pieces) == 1 else jnp.concatenate(pieces, axis=0)
        pieces = [held]
        for mask in masks:
            partner = [(i, i ^ mask) for i in range(visits)]
            pieces.append(lax.ppermute(held, "visits", partner))
    return pieces


def exchange_stages(visits):
    bits = [1 << i for i in range(visits.bit_length() - 2, 0, -1)]
    stages = []
    while len(bits) > 2:
        stages.append([bits[0] ^ bits[1] | 1])
        bits = bits[1:]
    if len(bits) == 2:
        stages.append([bits[0] ^ bits[1] | 1, bits[1] | 1, bits[0] | 1])
    elif bits:
        stages.append([bits[0] | 1])
    return stages + [[1]] if visits > 1 else stages


def on_chip(value):
    if value.size > ON_CHIP_LIMIT:
        return value
    return pltpu.with_memory_space_constraint(value, pltpu.VMEM)


def shards(exposure, patch_of, affine, psf_weights, psf_basis, detect_taps):
    visits = lax.axis_size("visits")
    tiles, height, extent = exposure.shape
    if visits > 256 or visits & (visits - 1):
        raise ValueError("visits")
    vmem = pl.BlockSpec(memory_space=pltpu.VMEM)
    smem = pl.BlockSpec(memory_space=pltpu.SMEM)
    anywhere = pl.BlockSpec(memory_space=pl.ANY)
    rows = block_rows(tiles, height)
    warped, block = pl.pallas_call(
        match_kernel,
        name="match",
        out_shape=(
            pltpu.VMEM(exposure.shape, jnp.float32),
            pltpu.VMEM((rows, extent), jnp.bfloat16),
        ),
        in_specs=[vmem, smem, smem, smem, smem],
        out_specs=(vmem, vmem),
    )(exposure, patch_of, affine, psf_weights, psf_basis)
    pieces = [on_chip(piece) for piece in gather_blocks(block, visits)]
    warped = on_chip(warped)
    results = (
        jax.ShapeDtypeStruct((1, height, extent), jnp.bfloat16),
        jax.ShapeDtypeStruct(exposure.shape, jnp.float32),
        jax.ShapeDtypeStruct(exposure.shape, jnp.float32),
    )
    scratch = [pltpu.VMEM(result.shape, result.dtype) for result in results]
    scratch.append(pltpu.SemaphoreType.DMA((3,)))
    strip = (height, extent)
    if len(pieces) != 2 or visits * tiles * (tiles + 1) > UNROLL_LIMIT:
        return pl.pallas_call(
            lambda *refs: coadd_kernel(len(pieces), *refs),
            name="coadd",
            out_shape=results,
            in_specs=[vmem] * len(pieces) + [smem, smem, smem, smem, vmem],
            out_specs=(anywhere, anywhere, anywhere),
            scratch_shapes=scratch
            + [pltpu.VMEM((visits,) + strip, jnp.float32), pltpu.VMEM((tiles + 1,) + strip, jnp.float32)],
        )(*pieces, patch_of, psf_weights, psf_basis, detect_taps, warped)
    rank, taps = psf_basis.shape[1:]
    ranked_shape = (tiles + 1, visits // 2) + strip
    prepared = pl.pallas_call(
        prep_kernel,
        name="prep",
        out_shape=tuple(
            pltpu.VMEM(shape + strip, jnp.float32)
            for shape in ((tiles + 1,), (rank, taps), (rank, taps), (rank, tiles), (taps,), (taps,))
        ),
        in_specs=[smem] * 4,
        out_specs=(vmem,) * 6,
    )(patch_of, psf_weights, psf_basis, detect_taps)
    prepared = [on_chip(value) for value in prepared]
    sifted = pl.pallas_call(
        sift_kernel,
        name="sift",
        out_shape=(pltpu.VMEM(ranked_shape, jnp.float32), pltpu.VMEM((tiles + 1,) + strip, jnp.float32)),
        in_specs=[vmem] * 2,
        out_specs=(vmem,) * 2,
    )(pieces[0], prepared[0])
    return pl.pallas_call(
        finish_kernel,
        name="finish",
        out_shape=results,
        in_specs=[vmem] * 10,
        out_specs=(anywhere, anywhere, anywhere),
        scratch_shapes=scratch + [pltpu.VMEM(ranked_shape, jnp.float32)],
    )(pieces[1], warped, *[on_chip(value) for value in sifted], *prepared)


def solution(mesh):
    placed = (
        P(("groups", "visits"), None, None),
        P(("groups", "visits")),
        P(None, ("groups", "visits")),
        P(None, None, ("groups", "visits")),
        P(),
        P(),
    )

    return jax.shard_map(
        shards,
        mesh=mesh,
        in_specs=placed,
        out_specs=(
            P(("groups", "visits"), None, None),
            P(("groups", "visits"), None, None),
            P(("groups", "visits"), None, None),
        ),
        check_vma=False,
    )
```

```python
import jax
import jax.numpy as jnp
from jax import lax
from jax.experimental import pallas as pl
from jax.experimental.pallas import tpu as pltpu
from jax.sharding import PartitionSpec as P


CHUNK = 7
UNROLL_LIMIT = 2048
ON_CHIP_LIMIT = 1 << 19


def round_up(value, step):
    return -(-value // step) * step


def block_rows(tiles, height):
    return round_up(tiles * height + round_up(tiles, height), 2 * height)


def reaches(taps, extent):
    centre = (taps - 1) // 2
    return [(p, p - centre) for p in range(taps) if abs(p - centre) < extent]


def col_tap_vector(value, reach, shape):
    cols = lax.broadcasted_iota(jnp.int32, shape, 1)
    inside = cols < shape[1] - reach if reach > 0 else cols >= -reach
    return jnp.where(inside, value, 0.0)


def row_tap_vector(value, reach, shape):
    rows = lax.broadcasted_iota(jnp.int32, shape, 0)
    inside = rows >= reach if reach > 0 else rows < shape[0] + reach
    return jnp.where(inside, value, 0.0)


def tap_filter(strips, rank, taps, row_tap, col_tap, weight):
    height, extent = strips[0].shape
    partial = [[None] * rank for _ in strips]
    for q, reach in reaches(taps, extent):
        scale = [col_tap(k, q, reach) for k in range(rank)]
        for e, strip in enumerate(strips):
            moved = pltpu.roll(strip, (-reach) % extent, 1) if reach else strip
            for k in range(rank):
                term = scale[k] * moved
                partial[e][k] = term if partial[e][k] is None else partial[e][k] + term
    if weight is not None:
        partial = [[weight(k, e) * partial[e][k] for k in range(rank)] for e in range(len(strips))]
    totals = [None] * len(strips)
    for p, reach in reaches(taps, height):
        scale = [row_tap(k, p, reach) for k in range(rank)]
        for e in range(len(strips)):
            mixed = scale[0] * partial[e][0]
            for k in range(1, rank):
                mixed = mixed + scale[k] * partial[e][k]
            if reach:
                mixed = pltpu.roll(mixed, (-reach) % height, 0)
            totals[e] = mixed if totals[e] is None else totals[e] + mixed
    return totals


def warp_strip(strip, coeff):
    height, extent = strip.shape
    rows = lax.broadcasted_iota(jnp.int32, (height, extent), 0)
    cols = lax.broadcasted_iota(jnp.int32, (height, extent), 1)
    src_row = jnp.clip((coeff(0) * rows + coeff(1) * cols + coeff(2)) >> 8, 0, height - 1)
    src_col = jnp.clip((coeff(3) * rows + coeff(4) * cols + coeff(5)) >> 8, 0, extent - 1)
    warped = jnp.zeros_like(strip)
    for r in range(height):
        line = jnp.broadcast_to(strip[r : r + 1, :], (height, extent))
        picked = jnp.take_along_axis(line, src_col, axis=1, mode="promise_in_bounds")
        warped = jnp.where(src_row == r, picked, warped)
    return warped


def match_kernel(*refs):
    sources, (warped_out, block_out), (sems, *held) = refs[:5], refs[5:7], refs[7:]
    copies = [pltpu.make_async_copy(sources[i], held[i], sems.at[i]) for i in range(5)]
    exposure, affine, psf_basis, psf_weights, patch_of = held
    for copy in copies:
        copy.start()
    tiles, height, extent = exposure.shape
    rank, taps = psf_basis.shape[1:]
    shape = (height, extent)
    pieces = []
    for first in range(0, tiles, CHUNK):
        chunk = range(first, min(first + CHUNK, tiles))
        if first == 0:
            copies[0].wait()
            copies[1].wait()
        strips = []
        for e in chunk:
            strips.append(warp_strip(exposure[e], lambda row, e=e: affine[row, e]))
            warped_out[e] = strips[-1]
        if first == 0:
            copies[2].wait()
            copies[3].wait()
        pieces += tap_filter(
            strips,
            rank,
            taps,
            lambda k, p, reach: row_tap_vector(psf_basis[0, k, p], reach, shape),
            lambda k, q, reach: col_tap_vector(psf_basis[1, k, q], reach, shape),
            lambda k, i, first=first: psf_weights[0, k, first + i],
        )
    copies[4].wait()
    rows = lax.broadcasted_iota(jnp.int32, shape, 0)
    for first in range(0, tiles, height):
        ids = jnp.full(shape, -1, jnp.int32)
        for t in range(first, min(first + height, tiles)):
            ids = jnp.where(rows == t - first, patch_of[t], ids)
        pieces.append(ids.astype(jnp.float32))
    while len(pieces) * height < block_out.shape[0]:
        pieces.append(jnp.full(shape, -1.0, jnp.float32))
    for i in range(0, len(pieces), 2):
        pair = jnp.concatenate(pieces[i : i + 2], axis=0)
        block_out[i * height : (i + 2) * height, :] = pair.astype(jnp.bfloat16)


def sorting_pairs(count):
    pairs = []
    p = 1
    while p < count:
        k = p
        while k >= 1:
            for j in range(k % p, count - k, 2 * k):
                for i in range(min(k, count - j - k)):
                    if (i + j) // (2 * p) == (i + j + k) // (2 * p):
                        pairs.append((i + j, i + j + k))
            k //= 2
        p *= 2
    return pairs


def fill_missing(candidates, fill):
    far = jnp.full(candidates[0].shape, jnp.inf, jnp.float32)
    values = []
    for value in candidates:
        missing = value == far
        values.append(jnp.where(missing, fill, value))
        fill = jnp.where(missing, -fill, fill)
    return values, fill


def sort_values(values):
    values = list(values)
    for low, high in sorting_pairs(len(values)):
        a, b = values[low], values[high]
        values[low], values[high] = jnp.minimum(a, b), jnp.maximum(a, b)
    return values


def middle(lower, upper, fill):
    upper = jnp.where(fill > 0, upper, lower)
    return ((lower + upper) * 0.5).astype(jnp.bfloat16).astype(jnp.float32)


def median_of(candidates):
    values, fill = fill_missing(candidates, jnp.full(candidates[0].shape, jnp.inf, jnp.float32))
    values = sort_values(values)
    return middle(values[len(values) // 2 - 1], values[len(values) // 2], fill)


def block_strips(block, at, tiles, height):
    parts = []
    for i in range(0, block_rows(tiles, height) // height, 2):
        pair = block[pl.ds(at + i * height, 2 * height), :].astype(jnp.float32)
        parts += [pair[:height], pair[height:]]
    return parts[:tiles], parts[tiles:]


def gather_candidates(block, at, targets, tiles):
    height, extent = targets[0].shape
    strips, ids = block_strips(block, at, tiles, height)
    found = [jnp.full((height, extent), jnp.inf, jnp.float32) for _ in targets]
    for t in range(tiles):
        row = t % height
        label = jnp.broadcast_to(ids[t // height][row : row + 1, :], (height, extent))
        for g, target in enumerate(targets):
            found[g] = jnp.where(label == target, strips[t], found[g])
    return found


def as_target(patch, shape):
    return jnp.full(shape, patch, jnp.int32).astype(jnp.float32)


def prep_kernel(
    patch_of, psf_weights, psf_basis, detect_taps, goals, cols, rows, weights, detect_cols, detect_rows
):
    n_targets, height, extent = goals.shape
    tiles = n_targets - 1
    rank, taps = psf_basis.shape[1:]
    shape = (height, extent)
    for t in range(tiles):
        goals[t] = as_target(patch_of[t], shape)
    goals[tiles] = as_target(lax.axis_index("visits"), shape)
    for q, reach in reaches(taps, extent):
        detect_cols[q] = col_tap_vector(detect_taps[1, q], reach, shape)
        for k in range(rank):
            cols[k, q] = col_tap_vector(psf_basis[1, k, q], reach, shape)
    for p, reach in reaches(taps, height):
        detect_rows[p] = row_tap_vector(detect_taps[0, p], reach, shape)
        for k in range(rank):
            rows[k, p] = row_tap_vector(psf_basis[0, k, p], reach, shape)
    for k in range(rank):
        for e in range(tiles):
            weights[k, e] = jnp.full(shape, psf_weights[1, k, e], jnp.float32)


def sift_kernel(block, goals, ranked, fills):
    n_targets, half, height, extent = ranked.shape
    targets = [goals[g] for g in range(n_targets)]
    rows_each = block.shape[0] // half
    for b in range(half):
        for g, value in enumerate(gather_candidates(block, b * rows_each, targets, n_targets - 1)):
            ranked[g, b] = value
    for g in range(n_targets):
        far = jnp.full((height, extent), jnp.inf, jnp.float32)
        values, fill = fill_missing([ranked[g, b] for b in range(half)], far)
        for b, value in enumerate(sort_values(values)):
            ranked[g, b] = value
        fills[g] = fill


def finish_kernel(
    block, warped, ranked, fills, goals, cols, rows, weights, detect_cols, detect_rows, *refs
):
    outputs, staged, sems, held = refs[:3], refs[3:6], refs[6], refs[7]
    template_out, difference_out, detection_out = staged
    copies = [pltpu.make_async_copy(staged[i], outputs[i], sems.at[i]) for i in range(3)]
    n_targets, half, _, _ = ranked.shape
    tiles = n_targets - 1
    rank, taps = cols.shape[:2]
    targets = [goals[g] for g in range(n_targets)]
    rows_each = block.shape[0] // half
    for b in range(half):
        for g, value in enumerate(gather_candidates(block, b * rows_each, targets, tiles)):
            held[g, b] = value
    models = []
    for g in range(n_targets):
        values, fill = fill_missing([held[g, b] for b in range(half)], fills[g])
        values = sort_values(values)
        lower, upper = None, None
        for b in range(half):
            first, second = ranked[g, b], values[half - 1 - b]
            low, high = jnp.minimum(first, second), jnp.maximum(first, second)
            lower = low if lower is None else jnp.maximum(lower, low)
            upper = high if upper is None else jnp.minimum(upper, high)
        models.append(middle(lower, upper, fill))
    template_out[0] = models[tiles].astype(jnp.bfloat16)
    copies[0].start()
    for first in range(0, tiles, CHUNK):
        chunk = range(first, min(first + CHUNK, tiles))
        modelled = tap_filter(
            [models[e] for e in chunk],
            rank,
            taps,
            lambda k, p, reach: rows[k, p],
            lambda k, q, reach: cols[k, q],
            lambda k, i, first=first: weights[k, first + i],
        )
        rest = []
        for i, e in enumerate(chunk):
            rest.append(jnp.where(targets[e] >= 0, warped[e] - modelled[i], 0.0))
            difference_out[e] = rest[-1]
        if chunk[-1] == tiles - 1:
            copies[1].start()
        detected = tap_filter(
            rest, 1, taps, lambda k, p, reach: detect_rows[p], lambda k, q, reach: detect_cols[q], None
        )
        for i, e in enumerate(chunk):
            detection_out[e] = detected[i]
    copies[2].start()
    for copy in copies:
        copy.wait()


def coadd_kernel(n_pieces, *refs):
    blocks = refs[:n_pieces]
    patch_of, psf_weights, psf_basis, detect_taps, warped = refs[n_pieces : n_pieces + 5]
    outputs = refs[n_pieces + 5 : n_pieces + 8]
    *staged, sems, held, models = refs[n_pieces + 8 :]
    template_out, difference_out, detection_out = staged
    copies = [pltpu.make_async_copy(staged[i], outputs[i], sems.at[i]) for i in range(3)]
    tiles, height, extent = warped.shape
    rank, taps = psf_basis.shape[1:]
    rows_each = block_rows(tiles, height)
    me = lax.axis_index("visits")
    visits = held.shape[0]

    def each_target(g, carry):
        patch = jnp.where(g < tiles, patch_of[jnp.minimum(g, tiles - 1)], me)
        target = [as_target(patch, (height, extent))]
        start = 0
        for block in blocks:

            def each_block(b, inner, block=block, start=start):
                at = pl.multiple_of(b * rows_each, 2 * height)
                held[start + b] = gather_candidates(block, at, target, tiles)[0]
                return inner

            count = block.shape[0] // rows_each
            lax.fori_loop(0, count, each_block, 0)
            start += count
        models[g] = median_of([held[s] for s in range(visits)])
        return carry

    lax.fori_loop(0, tiles + 1, each_target, 0)

    template_out[0] = models[tiles].astype(jnp.bfloat16)
    copies[0].start()
    for first in range(0, tiles, CHUNK):
        chunk = range(first, min(first + CHUNK, tiles))
        modelled = tap_filter(
            [models[e] for e in chunk],
            rank,
            taps,
            lambda k, p, reach: row_tap_vector(psf_basis[0, k, p], reach, (height, extent)),
            lambda k, q, reach: col_tap_vector(psf_basis[1, k, q], reach, (height, extent)),
            lambda k, i, first=first: psf_weights[1, k, first + i],
        )
        rest = []
        for i, e in enumerate(chunk):
            present = jnp.full((height, extent), patch_of[e], jnp.int32) >= 0
            rest.append(jnp.where(present, warped[e] - modelled[i], 0.0))
            difference_out[e] = rest[-1]
        if chunk[-1] == tiles - 1:
            copies[1].start()
        detected = tap_filter(
            rest,
            1,
            taps,
            lambda k, p, reach: row_tap_vector(detect_taps[0, p], reach, (height, extent)),
            lambda k, q, reach: col_tap_vector(detect_taps[1, q], reach, (height, extent)),
            None,
        )
        for i, e in enumerate(chunk):
            detection_out[e] = detected[i]
    copies[2].start()
    for copy in copies:
        copy.wait()


def gather_blocks(block, visits):
    if visits & (visits - 1):
        return [lax.all_gather(block, "visits", axis=0, tiled=True)]
    pieces = [block]
    for masks in exchange_stages(visits):
        held = pieces[0] if len(pieces) == 1 else jnp.concatenate(pieces, axis=0)
        pieces = [held]
        for mask in masks:
            partner = [(i, i ^ mask) for i in range(visits)]
            pieces.append(lax.ppermute(held, "visits", partner))
    return pieces


def exchange_stages(visits):
    bits = [1 << i for i in range(visits.bit_length() - 2, 0, -1)]
    stages = []
    while len(bits) > 2:
        stages.append([bits[0] ^ bits[1] | 1])
        bits = bits[1:]
    if len(bits) == 2:
        stages.append([bits[0] ^ bits[1] | 1, bits[1] | 1, bits[0] | 1])
    elif bits:
        stages.append([bits[0] | 1])
    return stages + [[1]] if visits > 1 else stages


def on_chip(value):
    if value.size > ON_CHIP_LIMIT:
        return value
    return pltpu.with_memory_space_constraint(value, pltpu.VMEM)


def shards(exposure, patch_of, affine, psf_weights, psf_basis, detect_taps):
    visits = lax.axis_size("visits")
    tiles, height, extent = exposure.shape
    if visits > 256 or visits & (visits - 1):
        raise ValueError("visits")
    vmem = pl.BlockSpec(memory_space=pltpu.VMEM)
    smem = pl.BlockSpec(memory_space=pltpu.SMEM)
    anywhere = pl.BlockSpec(memory_space=pl.ANY)
    rows = block_rows(tiles, height)
    warped, block = pl.pallas_call(
        match_kernel,
        name="match",
        out_shape=(
            pltpu.VMEM(exposure.shape, jnp.float32),
            pltpu.VMEM((rows, extent), jnp.bfloat16),
        ),
        in_specs=[anywhere] * 5,
        out_specs=(vmem, vmem),
        scratch_shapes=[
            pltpu.SemaphoreType.DMA((5,)),
            pltpu.VMEM(exposure.shape, exposure.dtype),
            *(pltpu.SMEM(value.shape, value.dtype) for value in (affine, psf_basis, psf_weights, patch_of)),
        ],
    )(exposure, affine, psf_basis, psf_weights, patch_of)
    pieces = [on_chip(piece) for piece in gather_blocks(block, visits)]
    warped = on_chip(warped)
    results = (
        jax.ShapeDtypeStruct((1, height, extent), jnp.bfloat16),
        jax.ShapeDtypeStruct(exposure.shape, jnp.float32),
        jax.ShapeDtypeStruct(exposure.shape, jnp.float32),
    )
    scratch = [pltpu.VMEM(result.shape, result.dtype) for result in results]
    scratch.append(pltpu.SemaphoreType.DMA((3,)))
    strip = (height, extent)
    if len(pieces) != 2 or visits * tiles * (tiles + 1) > UNROLL_LIMIT:
        return pl.pallas_call(
            lambda *refs: coadd_kernel(len(pieces), *refs),
            name="coadd",
            out_shape=results,
            in_specs=[vmem] * len(pieces) + [smem, smem, smem, smem, vmem],
            out_specs=(anywhere, anywhere, anywhere),
            scratch_shapes=scratch
            + [pltpu.VMEM((visits,) + strip, jnp.float32), pltpu.VMEM((tiles + 1,) + strip, jnp.float32)],
        )(*pieces, patch_of, psf_weights, psf_basis, detect_taps, warped)
    rank, taps = psf_basis.shape[1:]
    ranked_shape = (tiles + 1, visits // 2) + strip
    prepared = pl.pallas_call(
        prep_kernel,
        name="prep",
        out_shape=tuple(
            pltpu.VMEM(shape + strip, jnp.float32)
            for shape in ((tiles + 1,), (rank, taps), (rank, taps), (rank, tiles), (taps,), (taps,))
        ),
        in_specs=[smem] * 4,
        out_specs=(vmem,) * 6,
    )(patch_of, psf_weights, psf_basis, detect_taps)
    prepared = [on_chip(value) for value in prepared]
    sifted = pl.pallas_call(
        sift_kernel,
        name="sift",
        out_shape=(pltpu.VMEM(ranked_shape, jnp.float32), pltpu.VMEM((tiles + 1,) + strip, jnp.float32)),
        in_specs=[vmem] * 2,
        out_specs=(vmem,) * 2,
    )(pieces[0], prepared[0])
    return pl.pallas_call(
        finish_kernel,
        name="finish",
        out_shape=results,
        in_specs=[vmem] * 10,
        out_specs=(anywhere, anywhere, anywhere),
        scratch_shapes=scratch + [pltpu.VMEM(ranked_shape, jnp.float32)],
    )(pieces[1], warped, *[on_chip(value) for value in sifted], *prepared)


def solution(mesh):
    placed = (
        P(("groups", "visits"), None, None),
        P(("groups", "visits")),
        P(None, ("groups", "visits")),
        P(None, None, ("groups", "visits")),
        P(),
        P(),
    )

    return jax.shard_map(
        shards,
        mesh=mesh,
        in_specs=placed,
        out_specs=(
            P(("groups", "visits"), None, None),
            P(("groups", "visits"), None, None),
            P(("groups", "visits"), None, None),
        ),
        check_vma=False,
    )
```

```python
import jax
import jax.numpy as jnp
from jax import lax
from jax.experimental import pallas as pl
from jax.experimental.pallas import tpu as pltpu
from jax.sharding import PartitionSpec as P


CHUNK = 7
UNROLL_LIMIT = 2048
ON_CHIP_LIMIT = 1 << 19


def round_up(value, step):
    return -(-value // step) * step


def block_rows(tiles, height):
    return round_up(tiles * height + round_up(tiles, height), 2 * height)


def reaches(taps, extent):
    centre = (taps - 1) // 2
    return [(p, p - centre) for p in range(taps) if abs(p - centre) < extent]


def col_tap_vector(value, reach, shape):
    cols = lax.broadcasted_iota(jnp.int32, shape, 1)
    inside = cols < shape[1] - reach if reach > 0 else cols >= -reach
    return jnp.where(inside, value, 0.0)


def row_tap_vector(value, reach, shape):
    rows = lax.broadcasted_iota(jnp.int32, shape, 0)
    inside = rows >= reach if reach > 0 else rows < shape[0] + reach
    return jnp.where(inside, value, 0.0)


def tap_filter(strips, rank, taps, row_tap, col_tap, weight):
    _, extent = strips[0].shape
    partial = [[None] * rank for _ in strips]
    for q, reach in reaches(taps, extent):
        scale = [col_tap(k, q, reach) for k in range(rank)]
        for e, strip in enumerate(strips):
            moved = pltpu.roll(strip, (-reach) % extent, 1) if reach else strip
            for k in range(rank):
                term = scale[k] * moved
                partial[e][k] = term if partial[e][k] is None else partial[e][k] + term
    return mix_rows(partial, rank, taps, row_tap, weight)


def mix_rows(partial, rank, taps, row_tap, weight):
    height = partial[0][0].shape[0]
    if weight is not None:
        partial = [[weight(k, e) * partial[e][k] for k in range(rank)] for e in range(len(partial))]
    totals = [None] * len(partial)
    for p, reach in reaches(taps, height):
        scale = [row_tap(k, p, reach) for k in range(rank)]
        for e in range(len(partial)):
            mixed = scale[0] * partial[e][0]
            for k in range(1, rank):
                mixed = mixed + scale[k] * partial[e][k]
            if reach:
                mixed = pltpu.roll(mixed, (-reach) % height, 0)
            totals[e] = mixed if totals[e] is None else totals[e] + mixed
    return totals


def warp_strip(strip, coeff):
    height, extent = strip.shape
    rows = lax.broadcasted_iota(jnp.int32, (height, extent), 0)
    cols = lax.broadcasted_iota(jnp.int32, (height, extent), 1)
    src_row = jnp.clip((coeff(0) * rows + coeff(1) * cols + coeff(2)) >> 8, 0, height - 1)
    src_col = jnp.clip((coeff(3) * rows + coeff(4) * cols + coeff(5)) >> 8, 0, extent - 1)
    warped = jnp.zeros_like(strip)
    for r in range(height):
        line = jnp.broadcast_to(strip[r : r + 1, :], (height, extent))
        picked = jnp.take_along_axis(line, src_col, axis=1, mode="promise_in_bounds")
        warped = jnp.where(src_row == r, picked, warped)
    return warped


def match_kernel(*refs):
    sources, (warped_out, block_out), (sems, *held) = refs[:5], refs[5:7], refs[7:]
    copies = [pltpu.make_async_copy(sources[i], held[i], sems.at[i]) for i in range(5)]
    exposure, affine, psf_basis, psf_weights, patch_of = held
    for copy in copies:
        copy.start()
    tiles, height, extent = exposure.shape
    rank, taps = psf_basis.shape[1:]
    shape = (height, extent)
    pieces = []
    for first in range(0, tiles, CHUNK):
        chunk = range(first, min(first + CHUNK, tiles))
        if first == 0:
            copies[0].wait()
            copies[1].wait()
        strips = []
        for e in chunk:
            strips.append(warp_strip(exposure[e], lambda row, e=e: affine[row, e]))
            warped_out[e] = strips[-1]
        if first == 0:
            copies[2].wait()
            copies[3].wait()
        pieces += tap_filter(
            strips,
            rank,
            taps,
            lambda k, p, reach: row_tap_vector(psf_basis[0, k, p], reach, shape),
            lambda k, q, reach: col_tap_vector(psf_basis[1, k, q], reach, shape),
            lambda k, i, first=first: psf_weights[0, k, first + i],
        )
    copies[4].wait()
    rows = lax.broadcasted_iota(jnp.int32, shape, 0)
    for first in range(0, tiles, height):
        ids = jnp.full(shape, -1, jnp.int32)
        for t in range(first, min(first + height, tiles)):
            ids = jnp.where(rows == t - first, patch_of[t], ids)
        pieces.append(ids.astype(jnp.float32))
    while len(pieces) * height < block_out.shape[0]:
        pieces.append(jnp.full(shape, -1.0, jnp.float32))
    for i in range(0, len(pieces), 2):
        pair = jnp.concatenate(pieces[i : i + 2], axis=0)
        block_out[i * height : (i + 2) * height, :] = pair.astype(jnp.bfloat16)


def sorting_pairs(count):
    pairs = []
    p = 1
    while p < count:
        k = p
        while k >= 1:
            for j in range(k % p, count - k, 2 * k):
                for i in range(min(k, count - j - k)):
                    if (i + j) // (2 * p) == (i + j + k) // (2 * p):
                        pairs.append((i + j, i + j + k))
            k //= 2
        p *= 2
    return pairs


def fill_missing(candidates, fill):
    far = jnp.full(candidates[0].shape, jnp.inf, jnp.float32)
    values = []
    for value in candidates:
        missing = value == far
        values.append(jnp.where(missing, fill, value))
        fill = jnp.where(missing, -fill, fill)
    return values, fill


def sort_values(values):
    values = list(values)
    for low, high in sorting_pairs(len(values)):
        a, b = values[low], values[high]
        values[low], values[high] = jnp.minimum(a, b), jnp.maximum(a, b)
    return values


def middle(lower, upper, fill):
    upper = jnp.where(fill > 0, upper, lower)
    return ((lower + upper) * 0.5).astype(jnp.bfloat16).astype(jnp.float32)


def median_of(candidates):
    values, fill = fill_missing(candidates, jnp.full(candidates[0].shape, jnp.inf, jnp.float32))
    values = sort_values(values)
    return middle(values[len(values) // 2 - 1], values[len(values) // 2], fill)


def block_strips(block, at, tiles, height):
    parts = []
    for i in range(0, block_rows(tiles, height) // height, 2):
        pair = block[pl.ds(at + i * height, 2 * height), :].astype(jnp.float32)
        parts += [pair[:height], pair[height:]]
    return parts[:tiles], parts[tiles:]


def gather_candidates(block, at, targets, tiles):
    height, extent = targets[0].shape
    strips, ids = block_strips(block, at, tiles, height)
    found = [jnp.full((height, extent), jnp.inf, jnp.float32) for _ in targets]
    for t in range(tiles):
        row = t % height
        label = jnp.broadcast_to(ids[t // height][row : row + 1, :], (height, extent))
        for g, target in enumerate(targets):
            found[g] = jnp.where(label == target, strips[t], found[g])
    return found


def as_target(patch, shape):
    return jnp.full(shape, patch, jnp.int32).astype(jnp.float32)


def store_bands(bands, rank, taps, shape, tap):
    height, extent = shape
    row = lax.broadcasted_iota(jnp.int32, shape, 0)
    col = lax.broadcasted_iota(jnp.int32, shape, 1)
    centre = (taps - 1) // 2
    offset = row - col
    offset = jnp.where(offset < -centre, offset + extent, offset)
    heads = [jnp.zeros(shape, jnp.float32) for _ in range(rank)]
    for q, reach in reaches(taps, extent):
        here = offset == reach
        heads = [jnp.where(here, tap(k, q), heads[k]) for k in range(rank)]
    for at in range(0, extent, 2 * height):
        for k in range(rank):
            parts = []
            for top in (at, at + height):
                moved = pltpu.roll(heads[k], top, 1) if top else heads[k]
                parts.append(jnp.where(jnp.abs(row + top - col) <= centre, moved, 0.0))
            value = jnp.concatenate(parts, axis=0)
            high = value.astype(jnp.bfloat16)
            low = (value - high.astype(jnp.float32)).astype(jnp.bfloat16)
            lanes = slice(k * extent, (k + 1) * extent)
            bands[at : at + 2 * height, lanes] = high
            bands[extent + at : extent + at + 2 * height, lanes] = low


def prep_kernel(
    patch_of, psf_weights, psf_basis, detect_taps, goals, bands, rows, weights, detect_cols, detect_rows
):
    n_targets, height, extent = goals.shape
    tiles = n_targets - 1
    rank, taps = psf_basis.shape[1:]
    shape = (height, extent)
    for t in range(tiles):
        goals[t] = as_target(patch_of[t], shape)
    goals[tiles] = as_target(lax.axis_index("visits"), shape)
    for q, reach in reaches(taps, extent):
        detect_cols[q] = col_tap_vector(detect_taps[1, q], reach, shape)
    store_bands(bands, rank, taps, shape, lambda k, q: psf_basis[1, k, q])
    for p, reach in reaches(taps, height):
        detect_rows[p] = row_tap_vector(detect_taps[0, p], reach, shape)
        for k in range(rank):
            rows[k, p] = row_tap_vector(psf_basis[0, k, p], reach, shape)
    for k in range(rank):
        for e in range(tiles):
            weights[k, e] = jnp.full(shape, psf_weights[1, k, e], jnp.float32)


def sift_kernel(block, goals, ranked, fills):
    n_targets, half, height, extent = ranked.shape
    targets = [goals[g] for g in range(n_targets)]
    rows_each = block.shape[0] // half
    for b in range(half):
        for g, value in enumerate(gather_candidates(block, b * rows_each, targets, n_targets - 1)):
            ranked[g, b] = value
    for g in range(n_targets):
        far = jnp.full((height, extent), jnp.inf, jnp.float32)
        values, fill = fill_missing([ranked[g, b] for b in range(half)], far)
        for b, value in enumerate(sort_values(values)):
            ranked[g, b] = value
        fills[g] = fill


def finish_kernel(
    block, warped, ranked, fills, goals, bands, rows, weights, detect_cols, detect_rows, *refs
):
    outputs, staged, sems, held = refs[:3], refs[3:6], refs[6], refs[7]
    template_out, difference_out, detection_out = staged
    copies = [pltpu.make_async_copy(staged[i], outputs[i], sems.at[i]) for i in range(3)]
    n_targets, half, height, extent = ranked.shape
    tiles = n_targets - 1
    rank, taps = rows.shape[:2]
    targets = [goals[g] for g in range(n_targets)]
    rows_each = block.shape[0] // half
    for b in range(half):
        for g, value in enumerate(gather_candidates(block, b * rows_each, targets, tiles)):
            held[g, b] = value
    models = []
    for g in range(n_targets):
        values, fill = fill_missing([held[g, b] for b in range(half)], fills[g])
        values = sort_values(values)
        lower, upper = None, None
        for b in range(half):
            first, second = ranked[g, b], values[half - 1 - b]
            low, high = jnp.minimum(first, second), jnp.maximum(first, second)
            lower = low if lower is None else jnp.maximum(lower, low)
            upper = high if upper is None else jnp.minimum(upper, high)
        models.append(middle(lower, upper, fill))
    template_out[0] = models[tiles].astype(jnp.bfloat16)
    copies[0].start()
    stack = models + [jnp.zeros((height, extent), jnp.float32)] * (n_targets % 2)
    stack = jnp.concatenate(stack, axis=0).astype(jnp.bfloat16)
    spread = jnp.dot(
        jnp.concatenate([stack, stack], axis=1), bands[...], preferred_element_type=jnp.float32
    )
    partial = [
        [spread[e * height : (e + 1) * height, k * extent : (k + 1) * extent] for k in range(rank)]
        for e in range(tiles)
    ]
    modelled = mix_rows(partial, rank, taps, lambda k, p, reach: rows[k, p], lambda k, e: weights[k, e])
    rest = []
    for e in range(tiles):
        rest.append(jnp.where(targets[e] >= 0, warped[e] - modelled[e], 0.0))
        difference_out[e] = rest[-1]
    copies[1].start()
    detected = tap_filter(
        rest, 1, taps, lambda k, p, reach: detect_rows[p], lambda k, q, reach: detect_cols[q], None
    )
    for e in range(tiles):
        detection_out[e] = detected[e]
    copies[2].start()
    for copy in copies:
        copy.wait()


def coadd_kernel(n_pieces, *refs):
    blocks = refs[:n_pieces]
    patch_of, psf_weights, psf_basis, detect_taps, warped = refs[n_pieces : n_pieces + 5]
    outputs = refs[n_pieces + 5 : n_pieces + 8]
    *staged, sems, held, models = refs[n_pieces + 8 :]
    template_out, difference_out, detection_out = staged
    copies = [pltpu.make_async_copy(staged[i], outputs[i], sems.at[i]) for i in range(3)]
    tiles, height, extent = warped.shape
    rank, taps = psf_basis.shape[1:]
    rows_each = block_rows(tiles, height)
    me = lax.axis_index("visits")
    visits = held.shape[0]

    def each_target(g, carry):
        patch = jnp.where(g < tiles, patch_of[jnp.minimum(g, tiles - 1)], me)
        target = [as_target(patch, (height, extent))]
        start = 0
        for block in blocks:

            def each_block(b, inner, block=block, start=start):
                at = pl.multiple_of(b * rows_each, 2 * height)
                held[start + b] = gather_candidates(block, at, target, tiles)[0]
                return inner

            count = block.shape[0] // rows_each
            lax.fori_loop(0, count, each_block, 0)
            start += count
        models[g] = median_of([held[s] for s in range(visits)])
        return carry

    lax.fori_loop(0, tiles + 1, each_target, 0)

    template_out[0] = models[tiles].astype(jnp.bfloat16)
    copies[0].start()
    for first in range(0, tiles, CHUNK):
        chunk = range(first, min(first + CHUNK, tiles))
        modelled = tap_filter(
            [models[e] for e in chunk],
            rank,
            taps,
            lambda k, p, reach: row_tap_vector(psf_basis[0, k, p], reach, (height, extent)),
            lambda k, q, reach: col_tap_vector(psf_basis[1, k, q], reach, (height, extent)),
            lambda k, i, first=first: psf_weights[1, k, first + i],
        )
        rest = []
        for i, e in enumerate(chunk):
            present = jnp.full((height, extent), patch_of[e], jnp.int32) >= 0
            rest.append(jnp.where(present, warped[e] - modelled[i], 0.0))
            difference_out[e] = rest[-1]
        if chunk[-1] == tiles - 1:
            copies[1].start()
        detected = tap_filter(
            rest,
            1,
            taps,
            lambda k, p, reach: row_tap_vector(detect_taps[0, p], reach, (height, extent)),
            lambda k, q, reach: col_tap_vector(detect_taps[1, q], reach, (height, extent)),
            None,
        )
        for i, e in enumerate(chunk):
            detection_out[e] = detected[i]
    copies[2].start()
    for copy in copies:
        copy.wait()


def gather_blocks(block, visits):
    if visits & (visits - 1):
        return [lax.all_gather(block, "visits", axis=0, tiled=True)]
    pieces = [block]
    for masks in exchange_stages(visits):
        held = pieces[0] if len(pieces) == 1 else jnp.concatenate(pieces, axis=0)
        pieces = [held]
        for mask in masks:
            partner = [(i, i ^ mask) for i in range(visits)]
            pieces.append(lax.ppermute(held, "visits", partner))
    return pieces


def exchange_stages(visits):
    bits = [1 << i for i in range(visits.bit_length() - 2, 0, -1)]
    stages = []
    while len(bits) > 2:
        stages.append([bits[0] ^ bits[1] | 1])
        bits = bits[1:]
    if len(bits) == 2:
        stages.append([bits[0] ^ bits[1] | 1, bits[1] | 1, bits[0] | 1])
    elif bits:
        stages.append([bits[0] | 1])
    return stages + [[1]] if visits > 1 else stages


def on_chip(value):
    if value.size > ON_CHIP_LIMIT:
        return value
    return pltpu.with_memory_space_constraint(value, pltpu.VMEM)


def shards(exposure, patch_of, affine, psf_weights, psf_basis, detect_taps):
    visits = lax.axis_size("visits")
    tiles, height, extent = exposure.shape
    if visits > 256 or visits & (visits - 1):
        raise ValueError("visits")
    vmem = pl.BlockSpec(memory_space=pltpu.VMEM)
    smem = pl.BlockSpec(memory_space=pltpu.SMEM)
    anywhere = pl.BlockSpec(memory_space=pl.ANY)
    rows = block_rows(tiles, height)
    warped, block = pl.pallas_call(
        match_kernel,
        name="match",
        out_shape=(
            pltpu.VMEM(exposure.shape, jnp.float32),
            pltpu.VMEM((rows, extent), jnp.bfloat16),
        ),
        in_specs=[anywhere] * 5,
        out_specs=(vmem, vmem),
        scratch_shapes=[
            pltpu.SemaphoreType.DMA((5,)),
            pltpu.VMEM(exposure.shape, exposure.dtype),
            *(pltpu.SMEM(value.shape, value.dtype) for value in (affine, psf_basis, psf_weights, patch_of)),
        ],
    )(exposure, affine, psf_basis, psf_weights, patch_of)
    pieces = [on_chip(piece) for piece in gather_blocks(block, visits)]
    warped = on_chip(warped)
    results = (
        jax.ShapeDtypeStruct((1, height, extent), jnp.bfloat16),
        jax.ShapeDtypeStruct(exposure.shape, jnp.float32),
        jax.ShapeDtypeStruct(exposure.shape, jnp.float32),
    )
    scratch = [pltpu.VMEM(result.shape, result.dtype) for result in results]
    scratch.append(pltpu.SemaphoreType.DMA((3,)))
    strip = (height, extent)
    if len(pieces) != 2 or visits * tiles * (tiles + 1) > UNROLL_LIMIT:
        return pl.pallas_call(
            lambda *refs: coadd_kernel(len(pieces), *refs),
            name="coadd",
            out_shape=results,
            in_specs=[vmem] * len(pieces) + [smem, smem, smem, smem, vmem],
            out_specs=(anywhere, anywhere, anywhere),
            scratch_shapes=scratch
            + [pltpu.VMEM((visits,) + strip, jnp.float32), pltpu.VMEM((tiles + 1,) + strip, jnp.float32)],
        )(*pieces, patch_of, psf_weights, psf_basis, detect_taps, warped)
    rank, taps = psf_basis.shape[1:]
    ranked_shape = (tiles + 1, visits // 2) + strip
    prepared = pl.pallas_call(
        prep_kernel,
        name="prep",
        out_shape=tuple(
            pltpu.VMEM(shape, dtype)
            for shape, dtype in (
                ((tiles + 1,) + strip, jnp.float32),
                ((2 * extent, rank * extent), jnp.bfloat16),
                ((rank, taps) + strip, jnp.float32),
                ((rank, tiles) + strip, jnp.float32),
                ((taps,) + strip, jnp.float32),
                ((taps,) + strip, jnp.float32),
            )
        ),
        in_specs=[smem] * 4,
        out_specs=(vmem,) * 6,
    )(patch_of, psf_weights, psf_basis, detect_taps)
    prepared = [on_chip(value) for value in prepared]
    sifted = pl.pallas_call(
        sift_kernel,
        name="sift",
        out_shape=(pltpu.VMEM(ranked_shape, jnp.float32), pltpu.VMEM((tiles + 1,) + strip, jnp.float32)),
        in_specs=[vmem] * 2,
        out_specs=(vmem,) * 2,
    )(pieces[0], prepared[0])
    return pl.pallas_call(
        finish_kernel,
        name="finish",
        out_shape=results,
        in_specs=[vmem] * 10,
        out_specs=(anywhere, anywhere, anywhere),
        scratch_shapes=scratch + [pltpu.VMEM(ranked_shape, jnp.float32)],
    )(pieces[1], warped, *[on_chip(value) for value in sifted], *prepared)


def solution(mesh):
    placed = (
        P(("groups", "visits"), None, None),
        P(("groups", "visits")),
        P(None, ("groups", "visits")),
        P(None, None, ("groups", "visits")),
        P(),
        P(),
    )

    return jax.shard_map(
        shards,
        mesh=mesh,
        in_specs=placed,
        out_specs=(
            P(("groups", "visits"), None, None),
            P(("groups", "visits"), None, None),
            P(("groups", "visits"), None, None),
        ),
        check_vma=False,
    )
```

```python
import jax
import jax.numpy as jnp
from jax import lax
from jax.experimental import pallas as pl
from jax.experimental.pallas import tpu as pltpu
from jax.sharding import PartitionSpec as P


CHUNK = 7
UNROLL_LIMIT = 2048
ON_CHIP_LIMIT = 1 << 19
BAND_PARTS = 2


def round_up(value, step):
    return -(-value // step) * step


def block_rows(tiles, height):
    return round_up(tiles * height + round_up(tiles, height), 2 * height)


def reaches(taps, extent):
    centre = (taps - 1) // 2
    return [(p, p - centre) for p in range(taps) if abs(p - centre) < extent]


def col_tap_vector(value, reach, shape):
    cols = lax.broadcasted_iota(jnp.int32, shape, 1)
    inside = cols < shape[1] - reach if reach > 0 else cols >= -reach
    return jnp.where(inside, value, 0.0)


def row_tap_vector(value, reach, shape):
    rows = lax.broadcasted_iota(jnp.int32, shape, 0)
    inside = rows >= reach if reach > 0 else rows < shape[0] + reach
    return jnp.where(inside, value, 0.0)


def tap_filter(strips, rank, taps, row_tap, col_tap, weight):
    _, extent = strips[0].shape
    partial = [[None] * rank for _ in strips]
    for q, reach in reaches(taps, extent):
        scale = [col_tap(k, q, reach) for k in range(rank)]
        for e, strip in enumerate(strips):
            moved = pltpu.roll(strip, (-reach) % extent, 1) if reach else strip
            for k in range(rank):
                term = scale[k] * moved
                partial[e][k] = term if partial[e][k] is None else partial[e][k] + term
    return mix_rows(partial, rank, taps, row_tap, weight)


def mix_rows(partial, rank, taps, row_tap, weight):
    height = partial[0][0].shape[0]
    if weight is not None:
        partial = [[weight(k, e) * partial[e][k] for k in range(rank)] for e in range(len(partial))]
    totals = [None] * len(partial)
    for p, reach in reaches(taps, height):
        scale = [row_tap(k, p, reach) for k in range(rank)]
        for e in range(len(partial)):
            mixed = scale[0] * partial[e][0]
            for k in range(1, rank):
                mixed = mixed + scale[k] * partial[e][k]
            if reach:
                mixed = pltpu.roll(mixed, (-reach) % height, 0)
            totals[e] = mixed if totals[e] is None else totals[e] + mixed
    return totals


def warp_strip(strip, coeff):
    height, extent = strip.shape
    rows = lax.broadcasted_iota(jnp.int32, (height, extent), 0)
    cols = lax.broadcasted_iota(jnp.int32, (height, extent), 1)
    src_row = jnp.clip((coeff(0) * rows + coeff(1) * cols + coeff(2)) >> 8, 0, height - 1)
    src_col = jnp.clip((coeff(3) * rows + coeff(4) * cols + coeff(5)) >> 8, 0, extent - 1)
    warped = jnp.zeros_like(strip)
    for r in range(height):
        line = jnp.broadcast_to(strip[r : r + 1, :], (height, extent))
        picked = jnp.take_along_axis(line, src_col, axis=1, mode="promise_in_bounds")
        warped = jnp.where(src_row == r, picked, warped)
    return warped


def match_kernel(*refs):
    sources, (warped_out, block_out), (sems, *held) = refs[:5], refs[5:7], refs[7:]
    copies = [pltpu.make_async_copy(sources[i], held[i], sems.at[i]) for i in range(5)]
    exposure, affine, psf_basis, psf_weights, patch_of = held
    for copy in copies:
        copy.start()
    tiles, height, extent = exposure.shape
    rank, taps = psf_basis.shape[1:]
    shape = (height, extent)
    pieces = []
    for first in range(0, tiles, CHUNK):
        chunk = range(first, min(first + CHUNK, tiles))
        if first == 0:
            copies[0].wait()
            copies[1].wait()
        strips = []
        for e in chunk:
            strips.append(warp_strip(exposure[e], lambda row, e=e: affine[row, e]))
            warped_out[e] = strips[-1]
        if first == 0:
            copies[2].wait()
            copies[3].wait()
        pieces += tap_filter(
            strips,
            rank,
            taps,
            lambda k, p, reach: row_tap_vector(psf_basis[0, k, p], reach, shape),
            lambda k, q, reach: col_tap_vector(psf_basis[1, k, q], reach, shape),
            lambda k, i, first=first: psf_weights[0, k, first + i],
        )
    copies[4].wait()
    rows = lax.broadcasted_iota(jnp.int32, shape, 0)
    for first in range(0, tiles, height):
        ids = jnp.full(shape, -1, jnp.int32)
        for t in range(first, min(first + height, tiles)):
            ids = jnp.where(rows == t - first, patch_of[t], ids)
        pieces.append(ids.astype(jnp.float32))
    while len(pieces) * height < block_out.shape[0]:
        pieces.append(jnp.full(shape, -1.0, jnp.float32))
    for i in range(0, len(pieces), 2):
        pair = jnp.concatenate(pieces[i : i + 2], axis=0)
        block_out[i * height : (i + 2) * height, :] = pair.astype(jnp.bfloat16)


def sorting_pairs(count):
    pairs = []
    p = 1
    while p < count:
        k = p
        while k >= 1:
            for j in range(k % p, count - k, 2 * k):
                for i in range(min(k, count - j - k)):
                    if (i + j) // (2 * p) == (i + j + k) // (2 * p):
                        pairs.append((i + j, i + j + k))
            k //= 2
        p *= 2
    return pairs


def fill_missing(candidates, fill):
    far = jnp.full(candidates[0].shape, jnp.inf, jnp.float32)
    values = []
    for value in candidates:
        missing = value == far
        values.append(jnp.where(missing, fill, value))
        fill = jnp.where(missing, -fill, fill)
    return values, fill


def sort_values(values):
    values = list(values)
    for low, high in sorting_pairs(1 << (len(values) - 1).bit_length()):
        if high >= len(values):
            continue
        a, b = values[low], values[high]
        values[low], values[high] = jnp.minimum(a, b), jnp.maximum(a, b)
    return values


def merged(rank, first, second):
    best = None
    for j in range(max(0, rank + 1 - len(first)), min(len(second), rank + 1) + 1):
        i = rank + 1 - j
        ends = ([first[i - 1]] if i else []) + ([second[j - 1]] if j else [])
        top = ends[0] if len(ends) == 1 else jnp.maximum(*ends)
        best = top if best is None else jnp.minimum(best, top)
    return best


def needed(visits, late):
    half = visits // 2
    return range(max(0, half - 1 - late), min(half, visits - late - 1) + 1)


def middle(lower, upper, fill):
    upper = jnp.where(fill > 0, upper, lower)
    return ((lower + upper) * 0.5).astype(jnp.bfloat16).astype(jnp.float32)


def median_of(candidates):
    values, fill = fill_missing(candidates, jnp.full(candidates[0].shape, jnp.inf, jnp.float32))
    values = sort_values(values)
    return middle(values[len(values) // 2 - 1], values[len(values) // 2], fill)


def block_strips(block, at, tiles, height):
    parts = []
    for i in range(0, block_rows(tiles, height) // height, 2):
        pair = block[pl.ds(at + i * height, 2 * height), :].astype(jnp.float32)
        parts += [pair[:height], pair[height:]]
    return parts[:tiles], parts[tiles:]


def gather_candidates(block, at, targets, tiles):
    height, extent = targets[0].shape
    strips, ids = block_strips(block, at, tiles, height)
    found = [jnp.full((height, extent), jnp.inf, jnp.float32) for _ in targets]
    for t in range(tiles):
        row = t % height
        label = jnp.broadcast_to(ids[t // height][row : row + 1, :], (height, extent))
        for g, target in enumerate(targets):
            found[g] = jnp.where(label == target, strips[t], found[g])
    return found


def as_target(patch, shape):
    return jnp.full(shape, patch, jnp.int32).astype(jnp.float32)


def store_bands(bands, rank, taps, shape, tap):
    height, extent = shape
    row = lax.broadcasted_iota(jnp.int32, shape, 0)
    col = lax.broadcasted_iota(jnp.int32, shape, 1)
    centre = (taps - 1) // 2
    offset = row - col
    offset = jnp.where(offset < -centre, offset + extent, offset)
    heads = [jnp.zeros(shape, jnp.float32) for _ in range(rank)]
    for q, reach in reaches(taps, extent):
        here = offset == reach
        heads = [jnp.where(here, tap(k, q), heads[k]) for k in range(rank)]
    for at in range(0, extent, 2 * height):
        for k in range(rank):
            parts = []
            for top in (at, at + height):
                moved = pltpu.roll(heads[k], top, 1) if top else heads[k]
                parts.append(jnp.where(jnp.abs(row + top - col) <= centre, moved, 0.0))
            value = jnp.concatenate(parts, axis=0)
            lanes = slice(k * extent, (k + 1) * extent)
            for part in range(BAND_PARTS):
                rounded = value.astype(jnp.bfloat16)
                bands[part * extent + at : part * extent + at + 2 * height, lanes] = rounded
                value = value - rounded.astype(jnp.float32)


def prep_kernel(
    patch_of, psf_weights, psf_basis, detect_taps, goals, bands, rows, weights, detect_cols, detect_rows
):
    n_targets, height, extent = goals.shape
    tiles = n_targets - 1
    rank, taps = psf_basis.shape[1:]
    shape = (height, extent)
    for t in range(tiles):
        goals[t] = as_target(patch_of[t], shape)
    goals[tiles] = as_target(lax.axis_index("visits"), shape)
    for q, reach in reaches(taps, extent):
        detect_cols[q] = col_tap_vector(detect_taps[1, q], reach, shape)
    store_bands(bands, rank, taps, shape, lambda k, q: psf_basis[1, k, q])
    for p, reach in reaches(taps, height):
        detect_rows[p] = row_tap_vector(detect_taps[0, p], reach, shape)
        for k in range(rank):
            rows[k, p] = row_tap_vector(psf_basis[0, k, p], reach, shape)
    for k in range(rank):
        for e in range(tiles):
            weights[k, e] = jnp.full(shape, psf_weights[1, k, e], jnp.float32)


def sift_kernel(late, *refs):
    *blocks, goals, ranked, fills, held = refs
    n_targets, early, height, extent = held.shape
    tiles = n_targets - 1
    targets = [goals[g] for g in range(n_targets)]
    slot = 0
    for block in blocks:
        for at in range(0, block.shape[0], block_rows(tiles, height)):
            for g, value in enumerate(gather_candidates(block, at, targets, tiles)):
                held[g, slot] = value
            slot += 1
    for g in range(n_targets):
        far = jnp.full((height, extent), jnp.inf, jnp.float32)
        values, fill = fill_missing([held[g, b] for b in range(early)], far)
        values = sort_values(values)
        for i, r in enumerate(needed(early + late, late)):
            ranked[g, i] = values[r]
        fills[g] = fill


def finish_kernel(
    early, block, warped, ranked, fills, goals, bands, rows, weights, detect_cols, detect_rows, *refs
):
    outputs, staged, sems, held = refs[:3], refs[3:6], refs[6], refs[7]
    template_out, difference_out, detection_out = staged
    copies = [pltpu.make_async_copy(staged[i], outputs[i], sems.at[i]) for i in range(3)]
    n_targets, late, height, extent = held.shape
    tiles = n_targets - 1
    rank, taps = rows.shape[:2]
    targets = [goals[g] for g in range(n_targets)]
    rows_each = block_rows(tiles, height)
    visits = late + early
    for b in range(late):
        for g, value in enumerate(gather_candidates(block, b * rows_each, targets, tiles)):
            held[g, b] = value
    models = []
    for g in range(n_targets):
        values, fill = fill_missing([held[g, b] for b in range(late)], fills[g])
        values = sort_values(values)
        first = [None] * early
        for i, r in enumerate(needed(visits, late)):
            first[r] = ranked[g, i]
        half = visits // 2
        models.append(middle(merged(half - 1, first, values), merged(half, first, values), fill))
    template_out[0] = models[tiles].astype(jnp.bfloat16)
    copies[0].start()
    stack = models + [jnp.zeros((height, extent), jnp.float32)] * (n_targets % 2)
    stack = jnp.concatenate(stack, axis=0).astype(jnp.bfloat16)
    spread = jnp.dot(
        jnp.concatenate([stack] * BAND_PARTS, axis=1), bands[...], preferred_element_type=jnp.float32
    )
    partial = [
        [spread[e * height : (e + 1) * height, k * extent : (k + 1) * extent] for k in range(rank)]
        for e in range(tiles)
    ]
    modelled = mix_rows(partial, rank, taps, lambda k, p, reach: rows[k, p], lambda k, e: weights[k, e])
    rest = []
    for e in range(tiles):
        rest.append(jnp.where(targets[e] >= 0, warped[e] - modelled[e], 0.0))
        difference_out[e] = rest[-1]
    copies[1].start()
    detected = tap_filter(
        rest, 1, taps, lambda k, p, reach: detect_rows[p], lambda k, q, reach: detect_cols[q], None
    )
    for e in range(tiles):
        detection_out[e] = detected[e]
    copies[2].start()
    for copy in copies:
        copy.wait()


def coadd_kernel(n_pieces, *refs):
    blocks = refs[:n_pieces]
    patch_of, psf_weights, psf_basis, detect_taps, warped = refs[n_pieces : n_pieces + 5]
    outputs = refs[n_pieces + 5 : n_pieces + 8]
    *staged, sems, held, models = refs[n_pieces + 8 :]
    template_out, difference_out, detection_out = staged
    copies = [pltpu.make_async_copy(staged[i], outputs[i], sems.at[i]) for i in range(3)]
    tiles, height, extent = warped.shape
    rank, taps = psf_basis.shape[1:]
    rows_each = block_rows(tiles, height)
    me = lax.axis_index("visits")
    visits = held.shape[0]

    def each_target(g, carry):
        patch = jnp.where(g < tiles, patch_of[jnp.minimum(g, tiles - 1)], me)
        target = [as_target(patch, (height, extent))]
        start = 0
        for block in blocks:

            def each_block(b, inner, block=block, start=start):
                at = pl.multiple_of(b * rows_each, 2 * height)
                held[start + b] = gather_candidates(block, at, target, tiles)[0]
                return inner

            count = block.shape[0] // rows_each
            lax.fori_loop(0, count, each_block, 0)
            start += count
        models[g] = median_of([held[s] for s in range(visits)])
        return carry

    lax.fori_loop(0, tiles + 1, each_target, 0)

    template_out[0] = models[tiles].astype(jnp.bfloat16)
    copies[0].start()
    for first in range(0, tiles, CHUNK):
        chunk = range(first, min(first + CHUNK, tiles))
        modelled = tap_filter(
            [models[e] for e in chunk],
            rank,
            taps,
            lambda k, p, reach: row_tap_vector(psf_basis[0, k, p], reach, (height, extent)),
            lambda k, q, reach: col_tap_vector(psf_basis[1, k, q], reach, (height, extent)),
            lambda k, i, first=first: psf_weights[1, k, first + i],
        )
        rest = []
        for i, e in enumerate(chunk):
            present = jnp.full((height, extent), patch_of[e], jnp.int32) >= 0
            rest.append(jnp.where(present, warped[e] - modelled[i], 0.0))
            difference_out[e] = rest[-1]
        if chunk[-1] == tiles - 1:
            copies[1].start()
        detected = tap_filter(
            rest,
            1,
            taps,
            lambda k, p, reach: row_tap_vector(detect_taps[0, p], reach, (height, extent)),
            lambda k, q, reach: col_tap_vector(detect_taps[1, q], reach, (height, extent)),
            None,
        )
        for i, e in enumerate(chunk):
            detection_out[e] = detected[i]
    copies[2].start()
    for copy in copies:
        copy.wait()


def swap(held, visits, mask):
    return lax.ppermute(held, "visits", [(i, i ^ mask) for i in range(visits)])


def joined(pieces):
    return pieces[0] if len(pieces) == 1 else jnp.concatenate(pieces, axis=0)


def gather_blocks(block, visits, in_two):
    pieces = [block]
    *stages, last = exchange_stages(visits)
    for masks in stages:
        held = joined(pieces)
        pieces = [held]
        for mask in masks:
            pieces.append(swap(held, visits, mask))
    if not in_two or len(pieces) < 4:
        held = joined(pieces)
        return [held], swap(held, visits, last[0])
    soon, late = joined(pieces[:2]), joined(pieces[2:])
    return [soon, late, swap(soon, visits, last[0])], swap(late, visits, last[0])


def exchange_stages(visits):
    bits = [1 << i for i in range(visits.bit_length() - 2, 0, -1)]
    stages = []
    while len(bits) > 2:
        stages.append([bits[0] ^ bits[1] | 1])
        bits = bits[1:]
    if len(bits) == 2:
        stages.append([bits[0] ^ bits[1] | 1, bits[1] | 1, bits[0] | 1])
    elif bits:
        stages.append([bits[0] | 1])
    return stages + [[1]] if visits > 1 else stages


def on_chip(value):
    if value.size > ON_CHIP_LIMIT:
        return value
    return pltpu.with_memory_space_constraint(value, pltpu.VMEM)


def shards(exposure, patch_of, affine, psf_weights, psf_basis, detect_taps):
    visits = lax.axis_size("visits")
    tiles, height, extent = exposure.shape
    if visits > 256 or visits & (visits - 1):
        raise ValueError("visits")
    vmem = pl.BlockSpec(memory_space=pltpu.VMEM)
    smem = pl.BlockSpec(memory_space=pltpu.SMEM)
    anywhere = pl.BlockSpec(memory_space=pl.ANY)
    rows = block_rows(tiles, height)
    warped, block = pl.pallas_call(
        match_kernel,
        name="match",
        out_shape=(
            pltpu.VMEM(exposure.shape, jnp.float32),
            pltpu.VMEM((rows, extent), jnp.bfloat16),
        ),
        in_specs=[anywhere] * 5,
        out_specs=(vmem, vmem),
        scratch_shapes=[
            pltpu.SemaphoreType.DMA((5,)),
            pltpu.VMEM(exposure.shape, exposure.dtype),
            *(pltpu.SMEM(value.shape, value.dtype) for value in (affine, psf_basis, psf_weights, patch_of)),
        ],
    )(exposure, affine, psf_basis, psf_weights, patch_of)
    in_two = visits * tiles * (tiles + 1) <= UNROLL_LIMIT
    before, after = gather_blocks(block, visits, in_two)
    before, after = [on_chip(piece) for piece in before], on_chip(after)
    warped = on_chip(warped)
    results = (
        jax.ShapeDtypeStruct((1, height, extent), jnp.bfloat16),
        jax.ShapeDtypeStruct(exposure.shape, jnp.float32),
        jax.ShapeDtypeStruct(exposure.shape, jnp.float32),
    )
    scratch = [pltpu.VMEM(result.shape, result.dtype) for result in results]
    scratch.append(pltpu.SemaphoreType.DMA((3,)))
    strip = (height, extent)
    if not in_two:
        pieces = before + [after]
        return pl.pallas_call(
            lambda *refs: coadd_kernel(len(pieces), *refs),
            name="coadd",
            out_shape=results,
            in_specs=[vmem] * len(pieces) + [smem, smem, smem, smem, vmem],
            out_specs=(anywhere, anywhere, anywhere),
            scratch_shapes=scratch
            + [pltpu.VMEM((visits,) + strip, jnp.float32), pltpu.VMEM((tiles + 1,) + strip, jnp.float32)],
        )(*pieces, patch_of, psf_weights, psf_basis, detect_taps, warped)
    rank, taps = psf_basis.shape[1:]
    late = after.shape[0] // rows
    early = visits - late
    prepared = pl.pallas_call(
        prep_kernel,
        name="prep",
        out_shape=tuple(
            pltpu.VMEM(shape, dtype)
            for shape, dtype in (
                ((tiles + 1,) + strip, jnp.float32),
                ((BAND_PARTS * extent, rank * extent), jnp.bfloat16),
                ((rank, taps) + strip, jnp.float32),
                ((rank, tiles) + strip, jnp.float32),
                ((taps,) + strip, jnp.float32),
                ((taps,) + strip, jnp.float32),
            )
        ),
        in_specs=[smem] * 4,
        out_specs=(vmem,) * 6,
    )(patch_of, psf_weights, psf_basis, detect_taps)
    prepared = [on_chip(value) for value in prepared]
    sifted = pl.pallas_call(
        lambda *refs: sift_kernel(late, *refs),
        name="sift",
        out_shape=(
            pltpu.VMEM((tiles + 1, len(needed(visits, late))) + strip, jnp.float32),
            pltpu.VMEM((tiles + 1,) + strip, jnp.float32),
        ),
        in_specs=[vmem] * (len(before) + 1),
        out_specs=(vmem,) * 2,
        scratch_shapes=[pltpu.VMEM((tiles + 1, early) + strip, jnp.float32)],
    )(*before, prepared[0])
    return pl.pallas_call(
        lambda *refs: finish_kernel(early, *refs),
        name="finish",
        out_shape=results,
        in_specs=[vmem] * 10,
        out_specs=(anywhere, anywhere, anywhere),
        scratch_shapes=scratch + [pltpu.VMEM((tiles + 1, late) + strip, jnp.float32)],
    )(after, warped, *[on_chip(value) for value in sifted], *prepared)


def solution(mesh):
    placed = (
        P(("groups", "visits"), None, None),
        P(("groups", "visits")),
        P(None, ("groups", "visits")),
        P(None, None, ("groups", "visits")),
        P(),
        P(),
    )

    return jax.shard_map(
        shards,
        mesh=mesh,
        in_specs=placed,
        out_specs=(
            P(("groups", "visits"), None, None),
            P(("groups", "visits"), None, None),
            P(("groups", "visits"), None, None),
        ),
        check_vma=False,
    )
```

```python
import jax
import jax.numpy as jnp
from jax import lax
from jax.experimental import pallas as pl
from jax.experimental.pallas import tpu as pltpu
from jax.sharding import PartitionSpec as P


CHUNK = 7
UNROLL_LIMIT = 2048
ON_CHIP_LIMIT = 1 << 19
BAND_PARTS = 2


def round_up(value, step):
    return -(-value // step) * step


def block_rows(tiles, height):
    return round_up(tiles * height + round_up(tiles, height), 2 * height)


def reaches(taps, extent):
    centre = (taps - 1) // 2
    return [(p, p - centre) for p in range(taps) if abs(p - centre) < extent]


def col_tap_vector(value, reach, shape):
    cols = lax.broadcasted_iota(jnp.int32, shape, 1)
    inside = cols < shape[1] - reach if reach > 0 else cols >= -reach
    return jnp.where(inside, value, 0.0)


def row_tap_vector(value, reach, shape):
    rows = lax.broadcasted_iota(jnp.int32, shape, 0)
    inside = rows >= reach if reach > 0 else rows < shape[0] + reach
    return jnp.where(inside, value, 0.0)


def tap_filter(strips, rank, taps, row_tap, col_tap, weight):
    _, extent = strips[0].shape
    partial = [[None] * rank for _ in strips]
    for q, reach in reaches(taps, extent):
        scale = [col_tap(k, q, reach) for k in range(rank)]
        for e, strip in enumerate(strips):
            moved = pltpu.roll(strip, (-reach) % extent, 1) if reach else strip
            for k in range(rank):
                term = scale[k] * moved
                partial[e][k] = term if partial[e][k] is None else partial[e][k] + term
    return mix_rows(partial, rank, taps, row_tap, weight)


def mix_rows(partial, rank, taps, row_tap, weight):
    height = partial[0][0].shape[0]
    if weight is not None:
        partial = [[weight(k, e) * partial[e][k] for k in range(rank)] for e in range(len(partial))]
    totals = [None] * len(partial)
    for p, reach in reaches(taps, height):
        scale = [row_tap(k, p, reach) for k in range(rank)]
        for e in range(len(partial)):
            mixed = scale[0] * partial[e][0]
            for k in range(1, rank):
                mixed = mixed + scale[k] * partial[e][k]
            if reach:
                mixed = pltpu.roll(mixed, (-reach) % height, 0)
            totals[e] = mixed if totals[e] is None else totals[e] + mixed
    return totals


def warp_strip(strip, coeff):
    height, extent = strip.shape
    rows = lax.broadcasted_iota(jnp.int32, (height, extent), 0)
    cols = lax.broadcasted_iota(jnp.int32, (height, extent), 1)
    src_row = jnp.clip((coeff(0) * rows + coeff(1) * cols + coeff(2)) >> 8, 0, height - 1)
    src_col = jnp.clip((coeff(3) * rows + coeff(4) * cols + coeff(5)) >> 8, 0, extent - 1)
    warped = jnp.zeros_like(strip)
    for r in range(height):
        line = jnp.broadcast_to(strip[r : r + 1, :], (height, extent))
        picked = jnp.take_along_axis(line, src_col, axis=1, mode="promise_in_bounds")
        warped = jnp.where(src_row == r, picked, warped)
    return warped


def match_kernel(*refs):
    sources, (warped_out, block_out), (sems, *held) = refs[:5], refs[5:7], refs[7:]
    copies = [pltpu.make_async_copy(sources[i], held[i], sems.at[i]) for i in range(5)]
    exposure, affine, psf_basis, psf_weights, patch_of = held
    for i in (1, 0, 2, 3, 4):
        copies[i].start()
    tiles, height, extent = exposure.shape
    rank, taps = psf_basis.shape[1:]
    shape = (height, extent)
    pieces = []
    for first in range(0, tiles, CHUNK):
        chunk = range(first, min(first + CHUNK, tiles))
        if first == 0:
            copies[0].wait()
            copies[1].wait()
        strips = []
        for e in chunk:
            strips.append(warp_strip(exposure[e], lambda row, e=e: affine[row, e]))
            warped_out[e] = strips[-1]
        if first == 0:
            copies[2].wait()
            copies[3].wait()
        pieces += tap_filter(
            strips,
            rank,
            taps,
            lambda k, p, reach: row_tap_vector(psf_basis[0, k, p], reach, shape),
            lambda k, q, reach: col_tap_vector(psf_basis[1, k, q], reach, shape),
            lambda k, i, first=first: psf_weights[0, k, first + i],
        )
    copies[4].wait()
    rows = lax.broadcasted_iota(jnp.int32, shape, 0)
    for first in range(0, tiles, height):
        ids = jnp.full(shape, -1, jnp.int32)
        for t in range(first, min(first + height, tiles)):
            ids = jnp.where(rows == t - first, patch_of[t], ids)
        pieces.append(ids.astype(jnp.float32))
    while len(pieces) * height < block_out.shape[0]:
        pieces.append(jnp.full(shape, -1.0, jnp.float32))
    for i in range(0, len(pieces), 2):
        pair = jnp.concatenate(pieces[i : i + 2], axis=0)
        block_out[i * height : (i + 2) * height, :] = pair.astype(jnp.bfloat16)


def sorting_pairs(count):
    pairs = []
    p = 1
    while p < count:
        k = p
        while k >= 1:
            for j in range(k % p, count - k, 2 * k):
                for i in range(min(k, count - j - k)):
                    if (i + j) // (2 * p) == (i + j + k) // (2 * p):
                        pairs.append((i + j, i + j + k))
            k //= 2
        p *= 2
    return pairs


def fill_missing(candidates, fill):
    far = jnp.full(candidates[0].shape, jnp.inf, jnp.float32)
    values = []
    for value in candidates:
        missing = value == far
        values.append(jnp.where(missing, fill, value))
        fill = jnp.where(missing, -fill, fill)
    return values, fill


def sort_values(values):
    values = list(values)
    for low, high in sorting_pairs(1 << (len(values) - 1).bit_length()):
        if high >= len(values):
            continue
        a, b = values[low], values[high]
        values[low], values[high] = jnp.minimum(a, b), jnp.maximum(a, b)
    return values


def merged(rank, first, second):
    best = None
    for j in range(max(0, rank + 1 - len(first)), min(len(second), rank + 1) + 1):
        i = rank + 1 - j
        ends = ([first[i - 1]] if i else []) + ([second[j - 1]] if j else [])
        top = ends[0] if len(ends) == 1 else jnp.maximum(*ends)
        best = top if best is None else jnp.minimum(best, top)
    return best


def needed(visits, late):
    half = visits // 2
    return range(max(0, half - 1 - late), min(half, visits - late - 1) + 1)


def middle(lower, upper, fill):
    upper = jnp.where(fill > 0, upper, lower)
    return ((lower + upper) * 0.5).astype(jnp.bfloat16).astype(jnp.float32)


def median_of(candidates):
    values, fill = fill_missing(candidates, jnp.full(candidates[0].shape, jnp.inf, jnp.float32))
    values = sort_values(values)
    return middle(values[len(values) // 2 - 1], values[len(values) // 2], fill)


def block_strips(block, at, tiles, height):
    parts = []
    for i in range(0, block_rows(tiles, height) // height, 2):
        pair = block[pl.ds(at + i * height, 2 * height), :].astype(jnp.float32)
        parts += [pair[:height], pair[height:]]
    return parts[:tiles], parts[tiles:]


def gather_candidates(block, at, targets, tiles):
    height, extent = targets[0].shape
    strips, ids = block_strips(block, at, tiles, height)
    found = [jnp.full((height, extent), jnp.inf, jnp.float32) for _ in targets]
    for t in range(tiles):
        row = t % height
        label = jnp.broadcast_to(ids[t // height][row : row + 1, :], (height, extent))
        for g, target in enumerate(targets):
            found[g] = jnp.where(label == target, strips[t], found[g])
    return found


def as_target(patch, shape):
    return jnp.full(shape, patch, jnp.int32).astype(jnp.float32)


def store_bands(bands, rank, taps, shape, tap):
    height, extent = shape
    row = lax.broadcasted_iota(jnp.int32, shape, 0)
    col = lax.broadcasted_iota(jnp.int32, shape, 1)
    centre = (taps - 1) // 2
    offset = row - col
    offset = jnp.where(offset < -centre, offset + extent, offset)
    heads = [jnp.zeros(shape, jnp.float32) for _ in range(rank)]
    for q, reach in reaches(taps, extent):
        here = offset == reach
        heads = [jnp.where(here, tap(k, q), heads[k]) for k in range(rank)]
    for at in range(0, extent, 2 * height):
        for k in range(rank):
            parts = []
            for top in (at, at + height):
                moved = pltpu.roll(heads[k], top, 1) if top else heads[k]
                parts.append(jnp.where(jnp.abs(row + top - col) <= centre, moved, 0.0))
            value = jnp.concatenate(parts, axis=0)
            lanes = slice(k * extent, (k + 1) * extent)
            for part in range(BAND_PARTS):
                rounded = value.astype(jnp.bfloat16)
                bands[part * extent + at : part * extent + at + 2 * height, lanes] = rounded
                value = value - rounded.astype(jnp.float32)


def prep_kernel(
    patch_of, psf_weights, psf_basis, detect_taps, goals, bands, rows, weights, detect_cols, detect_rows
):
    n_targets, height, extent = goals.shape
    tiles = n_targets - 1
    rank, taps = psf_basis.shape[1:]
    shape = (height, extent)
    for t in range(tiles):
        goals[t] = as_target(patch_of[t], shape)
    goals[tiles] = as_target(lax.axis_index("visits"), shape)
    for q, reach in reaches(taps, extent):
        detect_cols[q] = col_tap_vector(detect_taps[1, q], reach, shape)
    store_bands(bands, rank, taps, shape, lambda k, q: psf_basis[1, k, q])
    for p, reach in reaches(taps, height):
        detect_rows[p] = row_tap_vector(detect_taps[0, p], reach, shape)
        for k in range(rank):
            rows[k, p] = row_tap_vector(psf_basis[0, k, p], reach, shape)
    for k in range(rank):
        for e in range(tiles):
            weights[k, e] = jnp.full(shape, psf_weights[1, k, e], jnp.float32)


def sift_kernel(late, *refs):
    *blocks, goals, ranked, fills, held = refs
    n_targets, early, height, extent = held.shape
    tiles = n_targets - 1
    targets = [goals[g] for g in range(n_targets)]
    slot = 0
    for block in blocks:
        for at in range(0, block.shape[0], block_rows(tiles, height)):
            for g, value in enumerate(gather_candidates(block, at, targets, tiles)):
                held[g, slot] = value
            slot += 1
    for g in range(n_targets):
        far = jnp.full((height, extent), jnp.inf, jnp.float32)
        values, fill = fill_missing([held[g, b] for b in range(early)], far)
        values = sort_values(values)
        for i, r in enumerate(needed(early + late, late)):
            ranked[g, i] = values[r]
        fills[g] = fill


def finish_kernel(
    early, block, warped, ranked, fills, goals, bands, rows, weights, detect_cols, detect_rows, *refs
):
    outputs, staged, sems, held = refs[:3], refs[3:6], refs[6], refs[7]
    template_out, difference_out, detection_out = staged
    copies = [pltpu.make_async_copy(staged[i], outputs[i], sems.at[i]) for i in range(3)]
    n_targets, late, height, extent = held.shape
    tiles = n_targets - 1
    rank, taps = rows.shape[:2]
    targets = [goals[g] for g in range(n_targets)]
    rows_each = block_rows(tiles, height)
    visits = late + early
    for b in range(late):
        for g, value in enumerate(gather_candidates(block, b * rows_each, targets, tiles)):
            held[g, b] = value
    models = []
    for g in range(n_targets):
        values, fill = fill_missing([held[g, b] for b in range(late)], fills[g])
        values = sort_values(values)
        first = [None] * early
        for i, r in enumerate(needed(visits, late)):
            first[r] = ranked[g, i]
        half = visits // 2
        models.append(middle(merged(half - 1, first, values), merged(half, first, values), fill))
    template_out[0] = models[tiles].astype(jnp.bfloat16)
    copies[0].start()
    stack = models + [jnp.zeros((height, extent), jnp.float32)] * (n_targets % 2)
    stack = jnp.concatenate(stack, axis=0).astype(jnp.bfloat16)
    spread = jnp.dot(
        jnp.concatenate([stack] * BAND_PARTS, axis=1), bands[...], preferred_element_type=jnp.float32
    )
    partial = [
        [spread[e * height : (e + 1) * height, k * extent : (k + 1) * extent] for k in range(rank)]
        for e in range(tiles)
    ]
    modelled = mix_rows(partial, rank, taps, lambda k, p, reach: rows[k, p], lambda k, e: weights[k, e])
    rest = []
    for e in range(tiles):
        rest.append(jnp.where(targets[e] >= 0, warped[e] - modelled[e], 0.0))
        difference_out[e] = rest[-1]
    copies[1].start()
    detected = tap_filter(
        rest, 1, taps, lambda k, p, reach: detect_rows[p], lambda k, q, reach: detect_cols[q], None
    )
    for e in range(tiles):
        detection_out[e] = detected[e]
    copies[2].start()
    for copy in copies:
        copy.wait()


def coadd_kernel(n_pieces, *refs):
    blocks = refs[:n_pieces]
    patch_of, psf_weights, psf_basis, detect_taps, warped = refs[n_pieces : n_pieces + 5]
    outputs = refs[n_pieces + 5 : n_pieces + 8]
    *staged, sems, held, models = refs[n_pieces + 8 :]
    template_out, difference_out, detection_out = staged
    copies = [pltpu.make_async_copy(staged[i], outputs[i], sems.at[i]) for i in range(3)]
    tiles, height, extent = warped.shape
    rank, taps = psf_basis.shape[1:]
    rows_each = block_rows(tiles, height)
    me = lax.axis_index("visits")
    visits = held.shape[0]

    def each_target(g, carry):
        patch = jnp.where(g < tiles, patch_of[jnp.minimum(g, tiles - 1)], me)
        target = [as_target(patch, (height, extent))]
        start = 0
        for block in blocks:

            def each_block(b, inner, block=block, start=start):
                at = pl.multiple_of(b * rows_each, 2 * height)
                held[start + b] = gather_candidates(block, at, target, tiles)[0]
                return inner

            count = block.shape[0] // rows_each
            lax.fori_loop(0, count, each_block, 0)
            start += count
        models[g] = median_of([held[s] for s in range(visits)])
        return carry

    lax.fori_loop(0, tiles + 1, each_target, 0)

    template_out[0] = models[tiles].astype(jnp.bfloat16)
    copies[0].start()
    for first in range(0, tiles, CHUNK):
        chunk = range(first, min(first + CHUNK, tiles))
        modelled = tap_filter(
            [models[e] for e in chunk],
            rank,
            taps,
            lambda k, p, reach: row_tap_vector(psf_basis[0, k, p], reach, (height, extent)),
            lambda k, q, reach: col_tap_vector(psf_basis[1, k, q], reach, (height, extent)),
            lambda k, i, first=first: psf_weights[1, k, first + i],
        )
        rest = []
        for i, e in enumerate(chunk):
            present = jnp.full((height, extent), patch_of[e], jnp.int32) >= 0
            rest.append(jnp.where(present, warped[e] - modelled[i], 0.0))
            difference_out[e] = rest[-1]
        if chunk[-1] == tiles - 1:
            copies[1].start()
        detected = tap_filter(
            rest,
            1,
            taps,
            lambda k, p, reach: row_tap_vector(detect_taps[0, p], reach, (height, extent)),
            lambda k, q, reach: col_tap_vector(detect_taps[1, q], reach, (height, extent)),
            None,
        )
        for i, e in enumerate(chunk):
            detection_out[e] = detected[i]
    copies[2].start()
    for copy in copies:
        copy.wait()


def swap(held, visits, partner):
    return lax.ppermute(held, "visits", [(i, partner(i)) for i in range(visits)])


def joined(pieces):
    return pieces[0] if len(pieces) == 1 else jnp.concatenate(pieces, axis=0)


def gather_blocks(block, visits, in_two):
    pieces = [block]
    *stages, last = exchange_stages(visits)
    for masks in stages:
        held = joined(pieces)
        pieces = [held]
        for partner in masks:
            pieces.append(swap(held, visits, partner))
    if not in_two or len(pieces) < 4:
        held = joined(pieces)
        return [held], swap(held, visits, last[0])
    soon, late = joined(pieces[:2]), joined(pieces[2:])
    return [soon, late, swap(soon, visits, last[0])], swap(late, visits, last[0])


def flip(mask):
    return lambda i: i ^ mask


def cross(top, below):
    return lambda i: i ^ (top | below | 1 if i & top else top | 1)


def exchange_stages(visits):
    bits = [1 << i for i in range(visits.bit_length() - 2, 0, -1)]
    stages = []
    while len(bits) > 2:
        stages.append([cross(bits[0], bits[1])])
        bits = bits[1:]
    if len(bits) == 2:
        stages.append([flip(bits[0] | bits[1] | 1), flip(bits[1] | 1), flip(bits[0] | 1)])
    elif bits:
        stages.append([flip(bits[0] | 1)])
    return stages + [[flip(1)]] if visits > 1 else stages


def on_chip(value):
    if value.size > ON_CHIP_LIMIT:
        return value
    return pltpu.with_memory_space_constraint(value, pltpu.VMEM)


def shards(exposure, patch_of, affine, psf_weights, psf_basis, detect_taps):
    visits = lax.axis_size("visits")
    tiles, height, extent = exposure.shape
    if visits > 256 or visits & (visits - 1):
        raise ValueError("visits")
    vmem = pl.BlockSpec(memory_space=pltpu.VMEM)
    smem = pl.BlockSpec(memory_space=pltpu.SMEM)
    anywhere = pl.BlockSpec(memory_space=pl.ANY)
    rows = block_rows(tiles, height)
    warped, block = pl.pallas_call(
        match_kernel,
        name="match",
        out_shape=(
            pltpu.VMEM(exposure.shape, jnp.float32),
            pltpu.VMEM((rows, extent), jnp.bfloat16),
        ),
        in_specs=[anywhere] * 5,
        out_specs=(vmem, vmem),
        scratch_shapes=[
            pltpu.SemaphoreType.DMA((5,)),
            pltpu.VMEM(exposure.shape, exposure.dtype),
            *(pltpu.SMEM(value.shape, value.dtype) for value in (affine, psf_basis, psf_weights, patch_of)),
        ],
    )(exposure, affine, psf_basis, psf_weights, patch_of)
    in_two = visits * tiles * (tiles + 1) <= UNROLL_LIMIT
    before, after = gather_blocks(block, visits, in_two)
    before, after = [on_chip(piece) for piece in before], on_chip(after)
    warped = on_chip(warped)
    results = (
        jax.ShapeDtypeStruct((1, height, extent), jnp.bfloat16),
        jax.ShapeDtypeStruct(exposure.shape, jnp.float32),
        jax.ShapeDtypeStruct(exposure.shape, jnp.float32),
    )
    scratch = [pltpu.VMEM(result.shape, result.dtype) for result in results]
    scratch.append(pltpu.SemaphoreType.DMA((3,)))
    strip = (height, extent)
    if not in_two:
        pieces = before + [after]
        return pl.pallas_call(
            lambda *refs: coadd_kernel(len(pieces), *refs),
            name="coadd",
            out_shape=results,
            in_specs=[vmem] * len(pieces) + [smem, smem, smem, smem, vmem],
            out_specs=(anywhere, anywhere, anywhere),
            scratch_shapes=scratch
            + [pltpu.VMEM((visits,) + strip, jnp.float32), pltpu.VMEM((tiles + 1,) + strip, jnp.float32)],
        )(*pieces, patch_of, psf_weights, psf_basis, detect_taps, warped)
    rank, taps = psf_basis.shape[1:]
    late = after.shape[0] // rows
    early = visits - late
    prepared = pl.pallas_call(
        prep_kernel,
        name="prep",
        out_shape=tuple(
            pltpu.VMEM(shape, dtype)
            for shape, dtype in (
                ((tiles + 1,) + strip, jnp.float32),
                ((BAND_PARTS * extent, rank * extent), jnp.bfloat16),
                ((rank, taps) + strip, jnp.float32),
                ((rank, tiles) + strip, jnp.float32),
                ((taps,) + strip, jnp.float32),
                ((taps,) + strip, jnp.float32),
            )
        ),
        in_specs=[smem] * 4,
        out_specs=(vmem,) * 6,
    )(patch_of, psf_weights, psf_basis, detect_taps)
    prepared = [on_chip(value) for value in prepared]
    sifted = pl.pallas_call(
        lambda *refs: sift_kernel(late, *refs),
        name="sift",
        out_shape=(
            pltpu.VMEM((tiles + 1, len(needed(visits, late))) + strip, jnp.float32),
            pltpu.VMEM((tiles + 1,) + strip, jnp.float32),
        ),
        in_specs=[vmem] * (len(before) + 1),
        out_specs=(vmem,) * 2,
        scratch_shapes=[pltpu.VMEM((tiles + 1, early) + strip, jnp.float32)],
    )(*before, prepared[0])
    return pl.pallas_call(
        lambda *refs: finish_kernel(early, *refs),
        name="finish",
        out_shape=results,
        in_specs=[vmem] * 10,
        out_specs=(anywhere, anywhere, anywhere),
        scratch_shapes=scratch + [pltpu.VMEM((tiles + 1, late) + strip, jnp.float32)],
    )(after, warped, *[on_chip(value) for value in sifted], *prepared)


def solution(mesh):
    placed = (
        P(("groups", "visits"), None, None),
        P(("groups", "visits")),
        P(None, ("groups", "visits")),
        P(None, None, ("groups", "visits")),
        P(),
        P(),
    )

    return jax.shard_map(
        shards,
        mesh=mesh,
        in_specs=placed,
        out_specs=(
            P(("groups", "visits"), None, None),
            P(("groups", "visits"), None, None),
            P(("groups", "visits"), None, None),
        ),
        check_vma=False,
    )
```
